256 devices in a mesh: dp: 16 (over y_lo, x, core), seq: 16 (over z, y_hi).
Axes of the slice: x: 4, y: 4 (y_hi: 2, y_lo: 2; y = y_hi * 2 + y_lo), z: 8, core: 2. Of those that a mesh axis runs over, the one named last changes fastest.
Arguments:
- student_in: bfloat16 [32768, 3584], P(('dp', 'seq')), may hold values from -24 to 24
- weight: bfloat16 [3584, 512], P(('dp', 'seq')), may hold values from -0.09375 to 0.09375
- queries: bfloat16 [32768, 512], P(('dp', 'seq')), may hold values from -8 to 8, as said below
- keys: bfloat16 [32768, 128], P(('dp', 'seq')), may hold values from -8 to 8
- values: bfloat16 [32768, 128], P(('dp', 'seq')), may hold values from -6 to 6
- lengths: int32 [16, 4], P('dp'), may hold values from 1 to 1536, 2048 in all within a row
- assignment: int32 [16, 16], P('dp'), may hold values from 0 to 15, each once within a row
Outputs:
- attention: bfloat16 [32768, 512], P(('dp', 'seq'))
- weight_grad: float32 [3584, 512], P(('dp', 'seq'))
The draws below stay inside these ranges and needn't reach their ends.
Inputs may be any that keep to these rules, and one draw needn't show every extreme that they name: `queries`: entries of head 0 and of keys may reach the ends of this range. Each row holds the lengths of 4 rollouts of one sequence, summing to 2048, the longest exactly 1536. `assignment`: each row is a permutation of the 16 rollout blocks of one sequence.
All inputs are finite; a program needn't handle non-finite values.
Results may differ from the reference program's by a relative error of at most 0.012.
Values may be sent and summed in bfloat16 or wider, within the bound.
No kernel may reach another device: no remote copies, remote signals or barrier semaphores. Data moves between devices by JAX's collectives and lax.ppermute only.
A program may use at most 64 MiB of HBM per device.

```python
import math
import jax
import jax.numpy as jnp
import numpy as np
from jax import lax

HD = 128
HQ = 4
DS = 3584
BLK = 128
DOCS = 4
SEQLEN = 2048
TOKENS_ALL = 32768
NBLK = 16
MAXLEN = 1536
N_DP = 16


def draw_queries(key, part):
    noise_key = jax.random.fold_in(key, 11)
    drawn = jnp.clip(jax.random.normal(noise_key, (TOKENS_ALL, HQ * HD), jnp.float32), -8.0, 8.0)
    return drawn.astype(jnp.bfloat16)


def draw_keys(key, part):
    noise_key = jax.random.fold_in(key, 13)
    drawn = jnp.clip(jax.random.normal(noise_key, (TOKENS_ALL, HD), jnp.float32), -8.0, 8.0)
    return drawn.astype(jnp.bfloat16)


def with_spikes(values, key, source, target, blocks, factor):
    def block_of(axis_at):
        return (jnp.arange(values.shape[axis_at]) // (values.shape[axis_at] // blocks)).reshape((-1,) + (1,) * (values.ndim - 1 - axis_at))

    first = jax.random.permutation(key, blocks)[block_of(target)]
    far = (block_of(target) + blocks // 2) % blocks
    return jnp.where((block_of(source) == first) | (block_of(source) == far), factor * values, values)


def block_scale(rng, dims, split, least, largest):
    gain = 1.0
    for dim, blocks in split:
        steps = jax.random.uniform(jax.random.fold_in(jax.random.fold_in(rng, 6), dim), (blocks,), jnp.float32, least / len(split), largest / len(split))
        gain = gain * jnp.repeat(jnp.exp(steps), dims[dim] // blocks).reshape((-1,) + (1,) * (len(dims) - 1 - dim))
    return gain


def split_up(amount, total, limit, lean):
    weights = [(1 << 20) // math.isqrt(grade ** lean) + 1 for grade in range(2, amount + 1)]
    rest, holding = total - limit - (amount - 1), [1] * (amount - 1)
    while rest > 0:
        candidates = [i for i in range(amount - 1) if holding[i] < limit]
        mass, left = sum([weights[i] for i in candidates]), rest
        for i in candidates:
            extra = min(limit - holding[i], max(1, left * weights[i] // mass), rest)
            holding[i] = holding[i] + extra
            rest = rest - extra
    return np.array([limit] + holding)


def uneven_parts(own_key, count, total, bound, lean):
    if count == 2:
        one = jax.random.randint(own_key, (), max(1, total - bound), min(bound, total - 1) + 1)
        return jnp.stack([one, total - one])
    sizes = jnp.asarray(split_up(count, total, bound, lean), jnp.int32)
    pairs = (count - 1) // 2
    donor, taker = sizes[1:1 + 2 * pairs:2], sizes[2:2 + 2 * pairs:2]
    slack = jnp.minimum(donor - 1, bound - taker)
    moved = jax.random.randint(jax.random.fold_in(own_key, 1), (pairs,), 0, 1 << 20) % (slack + 1)
    sizes = sizes.at[1:1 + 2 * pairs:2].set(donor - moved).at[2:2 + 2 * pairs:2].set(taker + moved)
    return sizes[jax.random.permutation(jax.random.fold_in(own_key, 2), count)]


def scatter_about(own_key, extent, scale, reach, cuts=(), kind=jnp.bfloat16):
    result = scale * jax.random.normal(own_key, extent, jnp.float32)
    if cuts:
        result = result * block_scale(own_key, extent, cuts, -0.22, 0.18)
    return jnp.clip(result, -reach, reach).astype(kind)


def bell_draw_with(own_key, shape, width, most, shards, heavy, kind=jnp.bfloat16):
    values = width * jax.random.normal(own_key, shape, jnp.float32)
    if shards:
        values = values * block_scale(own_key, shape, shards, -0.22, 0.18)
    return jnp.clip(with_spikes(values, jax.random.fold_in(own_key, 3), *heavy), -most, most).astype(kind)


def setup_inputs(seed: int = 0) -> dict:
    arg_keys = jax.random.split(jax.random.key(seed), 8)
    student_in = bell_draw_with(arg_keys[0], (TOKENS_ALL, DS), 1.0, 24.0, ((0, 256),), (0, 1, 256, 6.0))
    weight = scatter_about(arg_keys[1], (DS, HQ * HD), DS ** -0.5, 0.09375, ((0, 256),))
    queries = draw_queries(jax.random.fold_in(arg_keys[7], 71), 0)
    keys = draw_keys(jax.random.fold_in(arg_keys[7], 71), 0)
    values = scatter_about(arg_keys[4], (TOKENS_ALL, HD), 1.0, 6.0, ((0, 256),))
    lengths = jax.vmap(lambda own: uneven_parts(own, DOCS, SEQLEN, MAXLEN, 2))(jax.random.split(arg_keys[5], N_DP)).reshape((N_DP, DOCS)).astype(jnp.int32)
    assignment = jax.vmap(lambda own: jax.random.permutation(own, NBLK))(jax.random.split(arg_keys[6], N_DP)).reshape((N_DP, NBLK)).astype(jnp.int32)
    return {"student_in": student_in, "weight": weight, "queries": queries, "keys": keys, "values": values, "lengths": lengths, "assignment": assignment}


EPSILON = 1e-06
NEGATIVE = -1e+30

def locate(assign_row, length_row):
    slot_ids = jnp.arange(SEQLEN, dtype=jnp.int32)
    position = (assign_row[slot_ids // BLK] * BLK + slot_ids % BLK).astype(jnp.int32)
    doc_ends = jnp.cumsum(length_row).astype(jnp.int32)
    document = lax.optimization_barrier(jnp.sum((position[:, None] >= doc_ends[None, :]).astype(jnp.int32), axis=1))
    return (position, document)

def attend(query_rows, key_rows, value_rows, position, document):
    step_rows = math.gcd(SEQLEN, 512)
    blocks = query_rows.reshape(SEQLEN // step_rows, step_rows, HQ, HD)

    def one_block(block_items):
        query_block, query_pos, query_doc = block_items
        scores = jnp.einsum('qhd,kd->hqk', query_block.astype(jnp.float32), key_rows.astype(jnp.float32)) * HD ** (-0.5)
        allowed = (query_doc[:, None] == document[None, :]) & (query_pos[:, None] >= position[None, :])
        masked = jnp.where(allowed[None], scores, NEGATIVE)
        row_top = lax.optimization_barrier(jnp.max(masked, axis=-1, keepdims=True))
        exp_terms = jnp.where(allowed[None], jnp.exp(masked - row_top), 0.0)
        totals = lax.optimization_barrier(jnp.sum(exp_terms, axis=-1))
        rounded = lax.optimization_barrier(exp_terms.astype(jnp.bfloat16)).astype(jnp.float32)
        mixture = jnp.einsum('hqk,kd->qhd', rounded, value_rows.astype(jnp.float32))
        return (mixture / totals.T[:, :, None]).astype(jnp.bfloat16)
    attended = lax.map(one_block, (blocks, position.reshape(-1, step_rows), document.reshape(-1, step_rows)))
    return attended.reshape(SEQLEN, HQ * HD)

def reference(student_in, weight, queries, keys, values, lengths, assignment):

    def sequence(running, per_seq):
        rows_in, query_rows, key_rows, value_rows, length_row, assign_row = per_seq
        position, document = locate(assign_row, length_row)
        attended = attend(query_rows, key_rows, value_rows, position, document)
        as_float = rows_in.astype(jnp.float32)
        normed = (as_float * lax.rsqrt(lax.optimization_barrier(jnp.mean(as_float * as_float, axis=1, keepdims=True)) + EPSILON)).astype(jnp.bfloat16)
        predicted = jnp.dot(normed, weight, preferred_element_type=jnp.float32)
        scaled = ((predicted - attended.astype(jnp.float32)) * TOKENS_ALL ** (-0.5)).astype(jnp.bfloat16)
        partial_sum = lax.dot_general(normed, scaled, (((0,), (0,)), ((), ())), preferred_element_type=jnp.float32)
        return (running + partial_sum, attended)
    stacked = (student_in.reshape(N_DP, SEQLEN, DS), queries.reshape(N_DP, SEQLEN, HQ * HD), keys.reshape(N_DP, SEQLEN, HD), values.reshape(N_DP, SEQLEN, HD), lengths, assignment)
    weight_grad, attention = lax.scan(sequence, jnp.zeros((DS, HQ * HD), jnp.float32), stacked)
    return (attention.reshape(TOKENS_ALL, HQ * HD), weight_grad)
```

```python
import math

import jax
import jax.numpy as jnp
from jax import lax
from jax.sharding import Mesh, PartitionSpec as P

HD = 128
HQ = 4
BLK = 128
DS = 3584
COLS = HQ * HD
HALF = COLS // 2
TOKENS_ALL = 32768

EPSILON = 1e-06
NEGATIVE = -1e30

AXES = ("ylo", "x", "core", "z", "yhi")
SIZES = (2, 4, 2, 8, 2)
SEQ = ("z", "yhi")
WIDE = ("ylo", "x")
SWAP = ((0, 1), (1, 0))


def locate(assign_row, doc_ends, first_slot, count):
    slot_ids = first_slot + jnp.arange(count, dtype=jnp.int32)
    block_ids = slot_ids // BLK
    block_table = jnp.arange(assign_row.shape[0], dtype=jnp.int32)
    placed = jnp.sum(
        jnp.where(block_ids[:, None] == block_table[None, :], assign_row[None, :], 0), axis=1
    )
    position = placed * BLK + slot_ids % BLK
    document = jnp.sum((position[:, None] >= doc_ends[None, :]).astype(jnp.int32), axis=1)
    return (position, document)


def absorb_block(state, key_block, value_block, query_heads, allowed):
    run_max, run_total, run_acc = state
    scores = jnp.einsum(
        "qhd,kd->hqk", query_heads, key_block, preferred_element_type=jnp.float32
    ) * HD ** (-0.5)
    masked = jnp.where(allowed[None], scores, NEGATIVE)
    new_max = jnp.maximum(run_max, jnp.max(masked, axis=-1))
    fading = jnp.exp(run_max - new_max)
    exp_terms = jnp.where(allowed[None], jnp.exp(masked - new_max[:, :, None]), 0.0)
    new_total = run_total * fading + jnp.sum(exp_terms, axis=-1)
    mixture = jnp.einsum(
        "hqk,kd->qhd",
        exp_terms.astype(jnp.bfloat16),
        value_block,
        preferred_element_type=jnp.float32,
    )
    new_acc = run_acc * fading.T[:, :, None] + mixture
    return (new_max, new_total, new_acc)


def attend(queries, key_piece, value_piece, lengths, assignment):
    rows = queries.shape[0]
    assign_row = assignment[0]
    doc_ends = jnp.cumsum(lengths[0])
    query_pos, query_doc = locate(assign_row, doc_ends, lax.axis_index(SEQ) * rows, rows)
    query_heads = queries.reshape(rows, HQ, HD)
    start_state = (
        jnp.full((HQ, rows), NEGATIVE, jnp.float32),
        jnp.zeros((HQ, rows), jnp.float32),
        jnp.zeros((rows, HQ, HD), jnp.float32),
    )
    count = key_piece.shape[0]
    step_rows = math.gcd(count, 512)
    steps_count = count // step_rows
    key_pos, key_doc = locate(assign_row, doc_ends, jnp.int32(0), count)

    def one_step(running, slabs):
        key_block, value_block, key_position, key_document = slabs
        allowed = (query_doc[:, None] == key_document[None, :]) & (
            query_pos[:, None] >= key_position[None, :]
        )
        return (absorb_block(running, key_block, value_block, query_heads, allowed), None)

    slabs = (
        key_piece.reshape(steps_count, step_rows, HD),
        value_piece.reshape(steps_count, step_rows, HD),
        key_pos.reshape(steps_count, step_rows),
        key_doc.reshape(steps_count, step_rows),
    )
    result, _ = lax.scan(one_step, start_state, slabs)
    _, final_total, final_acc = result
    return (final_acc / final_total.T[:, :, None]).reshape(rows, COLS).astype(jnp.bfloat16)


def to_everyone(x, axes):
    size = math.prod(SIZES[AXES.index(a)] for a in axes)
    copies = jnp.broadcast_to(x, (size, *x.shape))
    return lax.all_to_all(copies, axes, split_axis=0, concat_axis=0, tiled=True)


def halves(x, core):
    low, high = x[:, :HALF], x[:, HALF:]
    return jnp.where(core == 0, low, high), jnp.where(core == 0, high, low)


def local(student_in, weight, queries, keys, values, lengths, assignment):
    rows = queries.shape[0]
    core = lax.axis_index("core")
    wrows = weight.shape[0]

    w_mine, w_other = halves(weight, core)
    w_got = lax.ppermute(w_other, "core", SWAP)
    w_first = jnp.where(core == 0, w_mine, w_got)
    w_second = jnp.where(core == 0, w_got, w_mine)
    kv = jnp.concatenate([keys, values], axis=1)
    pad = jnp.zeros((16 - wrows, HALF), jnp.bfloat16)
    packed = jnp.concatenate([kv, w_first, pad, w_second, pad], axis=0)
    arrived = to_everyone(packed, SEQ)

    as_float = student_in.astype(jnp.float32)
    normed = (
        as_float * lax.rsqrt(jnp.mean(as_float * as_float, axis=1, keepdims=True) + EPSILON)
    ).astype(jnp.bfloat16)
    both = jnp.concatenate([normed, lax.ppermute(normed, "core", SWAP)], axis=0)

    w_near = jnp.concatenate(
        [
            arrived[:, rows : rows + wrows].reshape(-1, HALF),
            arrived[:, rows + 16 : rows + 16 + wrows].reshape(-1, HALF),
        ],
        axis=0,
    )
    w_all = to_everyone(w_near, WIDE).reshape(DS, HALF)

    key_piece = arrived[:, :rows, :HD].reshape(-1, HD)
    value_piece = arrived[:, :rows, HD:].reshape(-1, HD)
    attention = attend(queries, key_piece, value_piece, lengths, assignment)
    a_mine, a_other = halves(attention, core)
    attended = jnp.concatenate([a_mine, lax.ppermute(a_other, "core", SWAP)], axis=0)

    predicted = jnp.dot(both, w_all, preferred_element_type=jnp.float32)
    scaled = ((predicted - attended.astype(jnp.float32)) * TOKENS_ALL ** (-0.5)).astype(
        jnp.bfloat16
    )
    part = lax.dot_general(
        both, scaled, (((0,), (0,)), ((), ())), preferred_element_type=jnp.float32
    ).astype(jnp.bfloat16)
    wide = lax.all_to_all(
        part.reshape(8, -1, HALF), WIDE, split_axis=0, concat_axis=0, tiled=True
    )
    near = wide.astype(jnp.float32).sum(axis=0).astype(jnp.bfloat16).reshape(32, wrows, HALF)
    last = lax.all_to_all(near, ("core", *SEQ), split_axis=0, concat_axis=0, tiled=True)
    summed = last.reshape(2, 16, wrows, HALF).astype(jnp.float32).sum(axis=1)
    weight_grad = jnp.concatenate([summed[0], summed[1]], axis=1)
    return (attention, weight_grad)


def solution(mesh):
    mesh = Mesh(mesh.devices.reshape(SIZES), AXES)
    token = P(AXES, None)
    row = P(("ylo", "x", "core"), None)
    return jax.shard_map(
        local,
        mesh=mesh,
        in_specs=(token, token, token, token, token, row, row),
        out_specs=(token, token),
        check_vma=False,
    )
```

```python
import math

import jax
import jax.numpy as jnp
from jax import lax
from jax.sharding import Mesh, PartitionSpec as P

HD = 128
HQ = 4
BLK = 128
DS = 3584
COLS = HQ * HD
HALF = COLS // 2
TOKENS_ALL = 32768

EPSILON = 1e-06
NEGATIVE = -1e30

AXES = ("ylo", "x", "core", "z", "yhi")
SIZES = (2, 4, 2, 8, 2)
SEQ = ("z", "yhi")
SWAP = ((0, 1), (1, 0))


def locate(assign_row, doc_ends, block_ids):
    block_table = jnp.arange(assign_row.shape[0], dtype=jnp.int32)
    placed = jnp.sum(
        jnp.where(block_ids[:, None] == block_table[None, :], assign_row[None, :], 0), axis=1
    )
    position = (placed[:, None] * BLK + jnp.arange(BLK, dtype=jnp.int32)[None, :]).reshape(-1)
    document = jnp.sum((position[:, None] >= doc_ends[None, :]).astype(jnp.int32), axis=1)
    return (position, document)


def absorb_block(state, key_block, value_block, query_heads, allowed):
    run_max, run_total, run_acc = state
    scores = jnp.einsum(
        "qhd,kd->hqk", query_heads, key_block, preferred_element_type=jnp.float32
    ) * HD ** (-0.5)
    masked = jnp.where(allowed[None], scores, NEGATIVE)
    new_max = jnp.maximum(run_max, jnp.max(masked, axis=-1))
    fading = jnp.exp(run_max - new_max)
    exp_terms = jnp.where(allowed[None], jnp.exp(masked - new_max[:, :, None]), 0.0)
    new_total = run_total * fading + jnp.sum(exp_terms, axis=-1)
    mixture = jnp.einsum(
        "hqk,kd->qhd",
        exp_terms.astype(jnp.bfloat16),
        value_block,
        preferred_element_type=jnp.float32,
    )
    new_acc = run_acc * fading.T[:, :, None] + mixture
    return (new_max, new_total, new_acc)


def attend(queries, key_piece, value_piece, block_ids, lengths, assignment):
    rows = queries.shape[0]
    assign_row = assignment[0]
    doc_ends = jnp.cumsum(lengths[0])
    query_pos, query_doc = locate(assign_row, doc_ends, lax.axis_index(SEQ)[None])
    query_heads = queries.reshape(rows, HQ, HD)
    start_state = (
        jnp.full((HQ, rows), NEGATIVE, jnp.float32),
        jnp.zeros((HQ, rows), jnp.float32),
        jnp.zeros((rows, HQ, HD), jnp.float32),
    )
    count = key_piece.shape[0]
    step_rows = math.gcd(count, 512)
    steps_count = count // step_rows
    key_pos, key_doc = locate(assign_row, doc_ends, block_ids)

    def one_step(running, slabs):
        key_block, value_block, key_position, key_document = slabs
        allowed = (query_doc[:, None] == key_document[None, :]) & (
            query_pos[:, None] >= key_position[None, :]
        )
        return (absorb_block(running, key_block, value_block, query_heads, allowed), None)

    slabs = (
        key_piece.reshape(steps_count, step_rows, HD),
        value_piece.reshape(steps_count, step_rows, HD),
        key_pos.reshape(steps_count, step_rows),
        key_doc.reshape(steps_count, step_rows),
    )
    result, _ = lax.scan(one_step, start_state, slabs)
    _, final_total, final_acc = result
    return (final_acc / final_total.T[:, :, None]).reshape(rows, COLS).astype(jnp.bfloat16)


def to_everyone(x, axes):
    size = math.prod(SIZES[AXES.index(a)] for a in axes)
    copies = jnp.broadcast_to(x, (size, *x.shape))
    return lax.all_to_all(copies, axes, split_axis=0, concat_axis=0, tiled=True)


def halves(x, which):
    half = x.shape[1] // 2
    low, high = x[:, :half], x[:, half:]
    return jnp.where(which == 0, low, high), jnp.where(which == 0, high, low)


def from_z(x, distance):
    return lax.ppermute(x, "z", [((i + distance) % 8, i) for i in range(8)])


def local(student_in, weight, queries, keys, values, lengths, assignment):
    rows = queries.shape[0]
    core = lax.axis_index("core")
    ylo = lax.axis_index("ylo")
    wrows = weight.shape[0]

    w_mine, w_other = halves(weight, core)
    w_got = lax.ppermute(w_other, "core", SWAP)
    kv = jnp.concatenate([keys, values], axis=1)
    kv_pair = jnp.concatenate([kv, lax.ppermute(kv, "yhi", SWAP)], axis=0)

    w_first = jnp.where(core == 0, w_mine, w_got)
    w_second = jnp.where(core == 0, w_got, w_mine)
    pad = jnp.zeros((16 - wrows, HALF), jnp.bfloat16)
    arrived = to_everyone(jnp.concatenate([w_first, pad, w_second, pad], axis=0), SEQ)

    as_float = student_in.astype(jnp.float32)
    normed = (
        as_float * lax.rsqrt(jnp.mean(as_float * as_float, axis=1, keepdims=True) + EPSILON)
    ).astype(jnp.bfloat16)
    n_keep, n_send = halves(normed, ylo)
    n_pair = jnp.concatenate([n_keep, lax.ppermute(n_send, "ylo", SWAP)], axis=0)
    n_all = jnp.concatenate([n_pair, lax.ppermute(n_pair, "core", SWAP)], axis=0)

    w_near = jnp.concatenate(
        [
            arrived[:, :wrows].reshape(-1, HALF),
            arrived[:, 16 : 16 + wrows].reshape(-1, HALF),
        ],
        axis=0,
    )
    w_near, n_all = lax.optimization_barrier((w_near, n_all))
    w_all = to_everyone(w_near, ("x",)).reshape(DS // 2, HALF)

    got = {d: from_z(kv_pair, d) for d in (3, -3, 2, -2, 1, -1)}
    got[0] = kv_pair
    got[4] = from_z(got[3], 1)
    order = sorted(got)
    pieces = lax.optimization_barrier(([got[d] for d in order], w_near))[0]
    kv_all = jnp.concatenate(pieces, axis=0)
    zs = (lax.axis_index("z") + jnp.array(order, jnp.int32)) % 8
    yhi = lax.axis_index("yhi")
    block_ids = (zs[:, None] * 2 + jnp.stack([yhi, 1 - yhi])[None, :]).reshape(-1)

    attention = attend(queries, kv_all[:, :HD], kv_all[:, HD:], block_ids, lengths, assignment)
    a_mine, a_other = halves(attention, core)
    a_got = lax.ppermute(a_other, "core", SWAP)

    partial = jnp.dot(n_all, w_all, preferred_element_type=jnp.float32)
    partial = partial.reshape(2, 2, rows, HALF)
    mine = partial[:, 0] - jnp.stack([a_mine, a_got]).astype(jnp.float32)
    theirs = partial[:, 1]
    back = lax.ppermute(jnp.stack([mine, theirs], axis=1).astype(jnp.bfloat16), "ylo", SWAP)
    back = back.astype(jnp.float32)
    diff = jnp.stack([mine + back[:, 1], theirs + back[:, 0]], axis=1)
    scaled = (diff * TOKENS_ALL ** (-0.5)).astype(jnp.bfloat16).reshape(4 * rows, HALF)
    part = lax.dot_general(
        n_all, scaled, (((0,), (0,)), ((), ())), preferred_element_type=jnp.float32
    ).astype(jnp.bfloat16)
    part = jnp.pad(part.reshape(-1, wrows, HALF), ((0, 0), (0, 16 - wrows), (0, 0)))
    last = lax.all_to_all(part, ("x", "core", *SEQ), split_axis=0, concat_axis=0, tiled=True)
    summed = last.reshape(4, 2, 16, 16, HALF).astype(jnp.float32).sum(axis=(0, 2))
    weight_grad = jnp.concatenate([summed[0, :wrows], summed[1, :wrows]], axis=1)
    return (attention, weight_grad)


def solution(mesh):
    mesh = Mesh(mesh.devices.reshape(SIZES), AXES)
    token = P(AXES, None)
    row = P(("ylo", "x", "core"), None)
    return jax.shard_map(
        local,
        mesh=mesh,
        in_specs=(token, token, token, token, token, row, row),
        out_specs=(token, token),
        check_vma=False,
    )
```

```python
import math

import jax
import jax.numpy as jnp
from jax import lax
from jax.experimental import pallas as pl
from jax.experimental.pallas import tpu as pltpu
from jax.sharding import Mesh, PartitionSpec as P

HD = 128
HQ = 4
BLK = 128
DS = 3584
COLS = HQ * HD
HALF = COLS // 2
TOKENS_ALL = 32768

EPSILON = 1e-06
NEGATIVE = -1e30
LOG2E = math.log2(math.e)

AXES = ("ylo", "x", "core", "z", "yhi")
SIZES = (2, 4, 2, 8, 2)
SEQ = ("z", "yhi")
SWAP = ((0, 1), (1, 0))


def attend_kernel(where_ref, assign_ref, length_ref, q_ref, kv_ref, out_ref, mine_ref, other_ref, s_ref):
    z, yhi, core = where_ref[0], where_ref[1], where_ref[2]
    rows = q_ref.shape[0]
    count = kv_ref.shape[0]
    chunk = 512
    per = chunk // BLK
    own = assign_ref[0, 2 * z + yhi] * BLK
    first = length_ref[0, 0]
    second = first + length_ref[0, 1]
    third = second + length_ref[0, 2]
    q_pos = own + lax.broadcasted_iota(jnp.int32, (rows, 1), 0)
    q_start = jnp.where(
        q_pos >= third,
        third,
        jnp.where(q_pos >= second, second, jnp.where(q_pos >= first, first, 0)),
    )
    q_all = jnp.concatenate([q_ref[:, h * HD : (h + 1) * HD] for h in range(HQ)], axis=0)
    lane = lax.broadcasted_iota(jnp.int32, (1, BLK), 1)
    top = None
    for c in range(count // chunk):
        k_pos = []
        for b in range(c * per, (c + 1) * per):
            slot = b // 2 * 2 + (yhi if b % 2 == 0 else 1 - yhi)
            k_pos.append(assign_ref[0, slot] * BLK + lane)
        k_pos = jnp.concatenate(k_pos, axis=1)
        bias = jnp.where((k_pos >= q_start) & (k_pos <= q_pos), 0.0, NEGATIVE)
        scores = lax.dot_general(
            q_all,
            kv_ref[c * chunk : (c + 1) * chunk, :HD],
            (((1,), (1,)), ((), ())),
            preferred_element_type=jnp.float32,
        )
        scores = scores.reshape(HQ, rows, chunk) * (HD ** (-0.5) * LOG2E) + bias[None]
        scores = scores.reshape(HQ * rows, chunk)
        s_ref[:, c * chunk : (c + 1) * chunk] = scores
        best = jnp.max(scores, axis=1, keepdims=True)
        top = best if top is None else jnp.maximum(top, best)
    total = jnp.zeros((HQ * rows, 1), jnp.float32)
    mixture = jnp.zeros((HQ * rows, HD), jnp.float32)
    for c in range(count // chunk):
        terms = jnp.exp2(s_ref[:, c * chunk : (c + 1) * chunk] - top)
        total = total + jnp.sum(terms, axis=1, keepdims=True)
        mixture = mixture + jnp.dot(
            terms.astype(jnp.bfloat16),
            kv_ref[c * chunk : (c + 1) * chunk, HD:],
            preferred_element_type=jnp.float32,
        )
    result = (mixture / total).astype(jnp.bfloat16)
    for h in range(HQ):
        head = result[h * rows : (h + 1) * rows]
        out_ref[:, h * HD : (h + 1) * HD] = head
        at = h % (HQ // 2) * HD

        @pl.when(core == h // (HQ // 2))
        def _():
            mine_ref[:, at : at + HD] = head

        @pl.when(core != h // (HQ // 2))
        def _():
            other_ref[:, at : at + HD] = head


def attend(queries, kv_all, lengths, assignment):
    rows = queries.shape[0]
    count = kv_all.shape[0]
    here = jnp.stack([lax.axis_index("z"), lax.axis_index("yhi"), lax.axis_index("core")])
    smem = pl.BlockSpec(memory_space=pltpu.SMEM)
    vmem = pl.BlockSpec(memory_space=pltpu.VMEM)
    half = jax.ShapeDtypeStruct((rows, HALF), jnp.bfloat16)
    return pl.pallas_call(
        attend_kernel,
        out_shape=(jax.ShapeDtypeStruct((rows, COLS), jnp.bfloat16), half, half),
        in_specs=[smem, smem, smem, vmem, vmem],
        out_specs=(vmem, vmem, vmem),
        scratch_shapes=[pltpu.VMEM((HQ * rows, count), jnp.float32)],
        compiler_params=pltpu.CompilerParams(vmem_limit_bytes=24 << 20),
        name="attend",
    )(here.astype(jnp.int32), assignment, lengths, queries, kv_all)


def to_everyone(x, axes):
    size = math.prod(SIZES[AXES.index(a)] for a in axes)
    copies = jnp.broadcast_to(x, (size, *x.shape))
    return lax.all_to_all(copies, axes, split_axis=0, concat_axis=0, tiled=True)


def halves(x, which):
    half = x.shape[1] // 2
    low, high = x[:, :half], x[:, half:]
    return jnp.where(which == 0, low, high), jnp.where(which == 0, high, low)


def local(student_in, weight, queries, keys, values, lengths, assignment):
    rows = queries.shape[0]
    core = lax.axis_index("core")
    ylo = lax.axis_index("ylo")
    wrows = weight.shape[0]

    w_mine, w_other = halves(weight, core)
    w_got = lax.ppermute(w_other, "core", SWAP)
    kv = jnp.concatenate([keys, values], axis=1)
    kv_pair = jnp.concatenate([kv, lax.ppermute(kv, "yhi", SWAP)], axis=0)
    kv_all = lax.all_gather(kv_pair, "z", axis=0, tiled=True)

    w_first = jnp.where(core == 0, w_mine, w_got)
    w_second = jnp.where(core == 0, w_got, w_mine)
    pad = jnp.zeros((16 - wrows, HALF), jnp.bfloat16)
    arrived = to_everyone(jnp.concatenate([w_first, pad, w_second, pad], axis=0), SEQ)

    as_float = student_in.astype(jnp.float32)
    normed = (
        as_float * lax.rsqrt(jnp.mean(as_float * as_float, axis=1, keepdims=True) + EPSILON)
    ).astype(jnp.bfloat16)
    n_keep, n_send = halves(normed, ylo)
    n_pair = jnp.concatenate([n_keep, lax.ppermute(n_send, "ylo", SWAP)], axis=0)
    n_all = jnp.concatenate([n_pair, lax.ppermute(n_pair, "core", SWAP)], axis=0)

    w_near = jnp.concatenate(
        [
            arrived[:, :wrows].reshape(-1, HALF),
            arrived[:, 16 : 16 + wrows].reshape(-1, HALF),
        ],
        axis=0,
    )
    w_near, n_all = lax.optimization_barrier((w_near, n_all))
    w_all = to_everyone(w_near, ("x",)).reshape(DS // 2, HALF)

    attention, a_mine, a_other = attend(queries, kv_all, lengths, assignment)
    a_got = lax.ppermute(a_other, "core", SWAP)

    partial = jnp.dot(n_all, w_all, preferred_element_type=jnp.float32)
    partial = partial.reshape(2, 2, rows, HALF)
    mine = partial[:, 0] - jnp.stack([a_mine, a_got]).astype(jnp.float32)
    theirs = partial[:, 1]
    back = lax.ppermute(jnp.stack([mine, theirs], axis=1).astype(jnp.bfloat16), "ylo", SWAP)
    back = back.astype(jnp.float32)
    diff = jnp.stack([mine + back[:, 1], theirs + back[:, 0]], axis=1)
    scaled = (diff * TOKENS_ALL ** (-0.5)).astype(jnp.bfloat16).reshape(4 * rows, HALF)
    part = lax.dot_general(
        n_all, scaled, (((0,), (0,)), ((), ())), preferred_element_type=jnp.float32
    ).astype(jnp.bfloat16)
    wide = lax.all_to_all(
        part.reshape(4, -1, HALF), "x", split_axis=0, concat_axis=0, tiled=True
    )
    near = wide.astype(jnp.float32).sum(axis=0).astype(jnp.bfloat16).reshape(-1, wrows, HALF)
    near = jnp.pad(near, ((0, 0), (0, 16 - wrows), (0, 0)))
    last = lax.all_to_all(near, ("core", *SEQ), split_axis=0, concat_axis=0, tiled=True)
    summed = last.reshape(2, 16, 16, HALF).astype(jnp.float32).sum(axis=1)
    weight_grad = jnp.concatenate([summed[0, :wrows], summed[1, :wrows]], axis=1)
    return (attention, weight_grad)


def solution(mesh):
    mesh = Mesh(mesh.devices.reshape(SIZES), AXES)
    token = P(AXES, None)
    row = P(("ylo", "x", "core"), None)
    return jax.shard_map(
        local,
        mesh=mesh,
        in_specs=(token, token, token, token, token, row, row),
        out_specs=(token, token),
        check_vma=False,
    )
```

```python
import math

import jax
import jax.numpy as jnp
from jax import lax
from jax.experimental import pallas as pl
from jax.experimental.pallas import tpu as pltpu
from jax.sharding import Mesh, PartitionSpec as P

HD = 128
HQ = 4
BLK = 128
COLS = HQ * HD
HALF = COLS // 2
TOKENS_ALL = 32768

EPSILON = 1e-06
NEGATIVE = -1e30
LOG2E = math.log2(math.e)

AXES = ("ylo", "x", "core", "z", "yhi")
SIZES = (2, 4, 2, 8, 2)
SEQ = ("z", "yhi")


def attend_kernel(where_ref, assign_ref, length_ref, q_ref, kv_ref, out_ref, mine_ref, other_ref, s_ref):
    slot, core = where_ref[0], where_ref[1]
    rows = q_ref.shape[0]
    count = kv_ref.shape[0]
    chunk = 512
    per = chunk // BLK
    own = assign_ref[0, slot] * BLK
    first = length_ref[0, 0]
    second = first + length_ref[0, 1]
    third = second + length_ref[0, 2]
    q_pos = own + lax.broadcasted_iota(jnp.int32, (rows, 1), 0)
    q_start = jnp.where(
        q_pos >= third,
        third,
        jnp.where(q_pos >= second, second, jnp.where(q_pos >= first, first, 0)),
    )
    q_all = jnp.concatenate([q_ref[:, h * HD : (h + 1) * HD] for h in range(HQ)], axis=0)
    lane = lax.broadcasted_iota(jnp.int32, (1, BLK), 1)
    top = None
    for c in range(count // chunk):
        k_pos = []
        for b in range(c * per, (c + 1) * per):
            k_pos.append(assign_ref[0, b] * BLK + lane)
        k_pos = jnp.concatenate(k_pos, axis=1)
        bias = jnp.where((k_pos >= q_start) & (k_pos <= q_pos), 0.0, NEGATIVE)
        scores = lax.dot_general(
            q_all,
            kv_ref[c * chunk : (c + 1) * chunk, :HD],
            (((1,), (1,)), ((), ())),
            preferred_element_type=jnp.float32,
        )
        scores = scores.reshape(HQ, rows, chunk) * (HD ** (-0.5) * LOG2E) + bias[None]
        scores = scores.reshape(HQ * rows, chunk)
        s_ref[:, c * chunk : (c + 1) * chunk] = scores
        best = jnp.max(scores, axis=1, keepdims=True)
        top = best if top is None else jnp.maximum(top, best)
    total = jnp.zeros((HQ * rows, 1), jnp.float32)
    mixture = jnp.zeros((HQ * rows, HD), jnp.float32)
    for c in range(count // chunk):
        terms = jnp.exp2(s_ref[:, c * chunk : (c + 1) * chunk] - top)
        total = total + jnp.sum(terms, axis=1, keepdims=True)
        mixture = mixture + jnp.dot(
            terms.astype(jnp.bfloat16),
            kv_ref[c * chunk : (c + 1) * chunk, HD:],
            preferred_element_type=jnp.float32,
        )
    result = (mixture / total).astype(jnp.bfloat16)
    for h in range(HQ):
        head = result[h * rows : (h + 1) * rows]
        out_ref[:, h * HD : (h + 1) * HD] = head
        at = h % (HQ // 2) * HD

        @pl.when(core == h // (HQ // 2))
        def _():
            mine_ref[:, at : at + HD] = head

        @pl.when(core != h // (HQ // 2))
        def _():
            other_ref[:, at : at + HD] = head


def attend(queries, kv_all, lengths, assignment):
    rows = queries.shape[0]
    count = kv_all.shape[0]
    here = jnp.stack([lax.axis_index(SEQ), lax.axis_index("core")])
    smem = pl.BlockSpec(memory_space=pltpu.SMEM)
    vmem = pl.BlockSpec(memory_space=pltpu.VMEM)
    half = jax.ShapeDtypeStruct((rows, HALF), jnp.bfloat16)
    return pl.pallas_call(
        attend_kernel,
        out_shape=(jax.ShapeDtypeStruct((rows, COLS), jnp.bfloat16), half, half),
        in_specs=[smem, smem, smem, vmem, vmem],
        out_specs=(vmem, vmem, vmem),
        scratch_shapes=[pltpu.VMEM((HQ * rows, count), jnp.float32)],
        compiler_params=pltpu.CompilerParams(vmem_limit_bytes=24 << 20),
        name="attend",
    )(here.astype(jnp.int32), assignment, lengths, queries, kv_all)


DOUBLING = (("z", 4, 3), ("yhi", 1, 0), ("z", 2, 2), ("z", 1, 1))


def arrange_kernel(where_ref, blocks_ref, out_ref):
    slot, core = where_ref[0], where_ref[1]
    wrows = out_ref.shape[0] // 32
    for c in range(2):
        for s in range(16):
            apart = lax.bitwise_xor(slot, s)
            at = 0
            for order, (_, _, bit) in enumerate(DOUBLING):
                at = at + lax.rem(apart // (1 << bit), 2) * (1 << order)
            block = blocks_ref[lax.bitwise_xor(core, c), at]
            first = (c * 16 + s) * wrows
            out_ref[first : first + wrows, :] = block[:wrows]


def arrange(blocks, wrows):
    here = jnp.stack([lax.axis_index(SEQ), lax.axis_index("core")])
    vmem = pl.BlockSpec(memory_space=pltpu.VMEM)
    return pl.pallas_call(
        arrange_kernel,
        out_shape=jax.ShapeDtypeStruct((32 * wrows, HALF), jnp.bfloat16),
        in_specs=[pl.BlockSpec(memory_space=pltpu.SMEM), vmem],
        out_specs=vmem,
        name="arrange",
    )(here.astype(jnp.int32), blocks)


def project_kernel(where_ref, n_ref, *refs):
    *w_refs, own_ref, send_ref, w_all = refs
    x = where_ref[0]
    step = w_refs[0].shape[0]
    for d, w_ref in enumerate(w_refs):
        at = lax.rem(x + d, len(w_refs)) * step
        w_all[pl.ds(pl.multiple_of(at, step), step), :] = w_ref[...]
    rows = n_ref.shape[0] // 4
    for b in range(4):
        part = jnp.dot(
            n_ref[b * rows : (b + 1) * rows, :], w_all[...], preferred_element_type=jnp.float32
        )
        own_ref[b * rows : (b + 1) * rows, :] = part
        t = b ^ 1
        send_ref[t * rows : (t + 1) * rows, :] = part.astype(jnp.bfloat16)


def project(n_all, pieces):
    here = jnp.stack([lax.axis_index("x")]).astype(jnp.int32)
    vmem = pl.BlockSpec(memory_space=pltpu.VMEM)
    shape = (n_all.shape[0], HALF)
    return pl.pallas_call(
        project_kernel,
        out_shape=(
            jax.ShapeDtypeStruct(shape, jnp.float32),
            jax.ShapeDtypeStruct(shape, jnp.bfloat16),
        ),
        in_specs=[pl.BlockSpec(memory_space=pltpu.SMEM)] + [vmem] * (1 + len(pieces)),
        out_specs=(vmem, vmem),
        scratch_shapes=[pltpu.VMEM((n_all.shape[1], HALF), jnp.bfloat16)],
        compiler_params=pltpu.CompilerParams(vmem_limit_bytes=16 << 20),
        name="project",
    )(here, n_all, *pieces)


def halves(x, which):
    half = x.shape[1] // 2
    low, high = x[:, :half], x[:, half:]
    return jnp.where(which == 0, low, high), jnp.where(which == 0, high, low)


def partner(x, axis, mask):
    size = SIZES[AXES.index(axis)]
    return lax.ppermute(x, axis, [(i, i ^ mask) for i in range(size)])


def local(student_in, weight, queries, keys, values, lengths, assignment):
    rows = queries.shape[0]
    core = lax.axis_index("core")
    ylo = lax.axis_index("ylo")
    wrows = weight.shape[0]

    kv = jnp.concatenate([keys, values], axis=1)
    kv_copies = jnp.broadcast_to(kv, (16, rows, 2 * HD))
    kv_all = lax.all_to_all(kv_copies, SEQ, split_axis=0, concat_axis=0, tiled=True)
    kv_all = kv_all.reshape(16 * rows, 2 * HD)

    w_mine, w_other = halves(weight, core)
    w_got = partner(w_other, "core", 1)
    blocks = jnp.pad(jnp.stack([w_mine, w_got])[:, None], ((0, 0), (0, 0), (0, 16 - wrows), (0, 0)))
    for axis, mask, _ in DOUBLING:
        blocks = jnp.concatenate([blocks, partner(blocks, axis, mask)], axis=1)
    w_near = arrange(blocks, wrows)
    pieces = [w_near]
    for d in range(1, 4):
        pieces.append(lax.ppermute(w_near, "x", [((i + d) % 4, i) for i in range(4)]))

    student_in, _, _ = lax.optimization_barrier((student_in, kv_copies, w_got))
    as_float = student_in.astype(jnp.float32)
    normed = (
        as_float * lax.rsqrt(jnp.mean(as_float * as_float, axis=1, keepdims=True) + EPSILON)
    ).astype(jnp.bfloat16)
    n_keep, n_send = halves(normed, ylo)
    n_pair = jnp.concatenate([n_keep, partner(n_send, "ylo", 1)], axis=0)
    n_all = jnp.concatenate([n_pair, partner(n_pair, "core", 1)], axis=0)

    own, send = project(n_all, pieces)
    back = partner(send, "ylo", 1)

    kv_all, _ = lax.optimization_barrier((kv_all, w_near))
    attention, a_mine, a_other = attend(queries, kv_all, lengths, assignment)
    attended = jnp.concatenate(
        [
            a_mine,
            partner(a_mine, "ylo", 1),
            partner(a_other, "core", 1),
            lax.ppermute(a_other, ("ylo", "core"), [(i, 3 - i) for i in range(4)]),
        ],
        axis=0,
    )

    diff = own + back.astype(jnp.float32) - attended.astype(jnp.float32)
    scaled = (diff * TOKENS_ALL ** (-0.5)).astype(jnp.bfloat16)
    part = lax.dot_general(
        n_all, scaled, (((0,), (0,)), ((), ())), preferred_element_type=jnp.float32
    ).astype(jnp.bfloat16)
    wide = lax.all_to_all(
        part.reshape(4, -1, HALF), "x", split_axis=0, concat_axis=0, tiled=True
    )
    near = wide.astype(jnp.float32).sum(axis=0).astype(jnp.bfloat16).reshape(-1, wrows, HALF)
    near = jnp.pad(near, ((0, 0), (0, 16 - wrows), (0, 0)))
    last = lax.all_to_all(near, ("core", *SEQ), split_axis=0, concat_axis=0, tiled=True)
    summed = last.reshape(2, 16, 16, HALF).astype(jnp.float32).sum(axis=1)
    weight_grad = jnp.concatenate([summed[0, :wrows], summed[1, :wrows]], axis=1)
    return (attention, weight_grad)


def solution(mesh):
    mesh = Mesh(mesh.devices.reshape(SIZES), AXES)
    token = P(AXES, None)
    row = P(("ylo", "x", "core"), None)
    return jax.shard_map(
        local,
        mesh=mesh,
        in_specs=(token, token, token, token, token, row, row),
        out_specs=(token, token),
        check_vma=False,
    )
```

```python
import math

import jax
import jax.numpy as jnp
from jax import lax
from jax.experimental import pallas as pl
from jax.experimental.pallas import tpu as pltpu
from jax.sharding import Mesh, PartitionSpec as P

HD = 128
HQ = 4
BLK = 128
COLS = HQ * HD
HALF = COLS // 2
TOKENS_ALL = 32768

EPSILON = 1e-06
NEGATIVE = -1e30
LOG2E = math.log2(math.e)

AXES = ("ylo", "x", "core", "z", "yhi")
SIZES = (2, 4, 2, 8, 2)
SEQ = ("z", "yhi")


RING = (0, 1, 2, 3, 4, -3, -2, -1)


def attend_kernel(where_ref, assign_ref, length_ref, q_ref, *refs):
    *kv_refs, out_ref, mine_ref, other_ref, s_ref = refs
    z, yhi, core = where_ref[0], where_ref[1], where_ref[2]
    rows = q_ref.shape[0]
    step = kv_refs[0].shape[0] // 2
    own = assign_ref[0, 2 * z + yhi] * BLK
    first = length_ref[0, 0]
    second = first + length_ref[0, 1]
    third = second + length_ref[0, 2]
    q_pos = own + lax.broadcasted_iota(jnp.int32, (rows, 1), 0)
    q_start = jnp.where(
        q_pos >= third,
        third,
        jnp.where(q_pos >= second, second, jnp.where(q_pos >= first, first, 0)),
    )
    q_all = jnp.concatenate([q_ref[:, h * HD : (h + 1) * HD] for h in range(HQ)], axis=0)
    lane = lax.broadcasted_iota(jnp.int32, (1, BLK), 1)
    chunk = 2 * BLK
    top = None
    for c, (distance, kv_ref) in enumerate(zip(RING, kv_refs)):
        pair = lax.rem(z + distance + 8, 8) * 2
        k_pos = [assign_ref[0, pair + yhi] * BLK + lane, assign_ref[0, pair + 1 - yhi] * BLK + lane]
        k_pos = jnp.concatenate(k_pos, axis=1)
        bias = jnp.where((k_pos >= q_start) & (k_pos <= q_pos), 0.0, NEGATIVE)
        k = jnp.concatenate([kv_ref[:BLK, :HD], kv_ref[step : step + BLK, :HD]], axis=0)
        scores = lax.dot_general(
            q_all, k, (((1,), (1,)), ((), ())), preferred_element_type=jnp.float32
        )
        scores = scores.reshape(HQ, rows, chunk) * (HD ** (-0.5) * LOG2E) + bias[None]
        scores = scores.reshape(HQ * rows, chunk)
        s_ref[:, c * chunk : (c + 1) * chunk] = scores
        best = jnp.max(scores, axis=1, keepdims=True)
        top = best if top is None else jnp.maximum(top, best)
    total = jnp.zeros((HQ * rows, 1), jnp.float32)
    mixture = jnp.zeros((HQ * rows, HD), jnp.float32)
    for c, kv_ref in enumerate(kv_refs):
        terms = jnp.exp2(s_ref[:, c * chunk : (c + 1) * chunk] - top)
        total = total + jnp.sum(terms, axis=1, keepdims=True)
        v = jnp.concatenate([kv_ref[:BLK, HD:], kv_ref[step : step + BLK, HD:]], axis=0)
        mixture = mixture + jnp.dot(
            terms.astype(jnp.bfloat16), v, preferred_element_type=jnp.float32
        )
    result = (mixture / total).astype(jnp.bfloat16)
    for h in range(HQ):
        head = result[h * rows : (h + 1) * rows]
        out_ref[:, h * HD : (h + 1) * HD] = head
        at = h % (HQ // 2) * HD

        @pl.when(core == h // (HQ // 2))
        def _():
            mine_ref[:, at : at + HD] = head

        @pl.when(core != h // (HQ // 2))
        def _():
            other_ref[:, at : at + HD] = head


def attend(here, queries, parts, lengths, assignment):
    rows = queries.shape[0]
    smem = pl.BlockSpec(memory_space=pltpu.SMEM)
    vmem = pl.BlockSpec(memory_space=pltpu.VMEM)
    half = jax.ShapeDtypeStruct((rows, HALF), jnp.bfloat16)
    return pl.pallas_call(
        attend_kernel,
        out_shape=(jax.ShapeDtypeStruct((rows, COLS), jnp.bfloat16), half, half),
        in_specs=[smem, smem, smem, vmem] + [vmem] * len(parts),
        out_specs=(vmem, vmem, vmem),
        scratch_shapes=[pltpu.VMEM((HQ * rows, 16 * BLK), jnp.float32)],
        compiler_params=pltpu.CompilerParams(vmem_limit_bytes=20 << 20),
        name="attend",
    )(here, assignment, lengths, queries, *parts)


def arrange_kernel(where_ref, *refs):
    *parts, out_ref, held = refs
    z, yhi, core = where_ref[0], where_ref[1], where_ref[2]
    wrows = out_ref.shape[0] // 32
    step = parts[0].shape[0] // 2
    for distance, part in zip(RING, parts):
        pair = lax.rem(z + distance + 8, 8) * 2
        for t in range(2):
            slot = pair + (yhi if t == 0 else 1 - yhi)
            for c in range(2):
                first = t * step + BLK + 16 * c
                held[lax.bitwise_xor(core, c), slot] = part[first : first + 16, :]
    for c in range(2):
        for s in range(16):
            first = (c * 16 + s) * wrows
            out_ref[first : first + wrows, :] = held[c, s, :wrows]


def arrange(here, parts, wrows):
    vmem = pl.BlockSpec(memory_space=pltpu.VMEM)
    return pl.pallas_call(
        arrange_kernel,
        out_shape=jax.ShapeDtypeStruct((32 * wrows, HALF), jnp.bfloat16),
        in_specs=[pl.BlockSpec(memory_space=pltpu.SMEM)] + [vmem] * len(parts),
        out_specs=vmem,
        scratch_shapes=[pltpu.VMEM((2, 16, 16, HALF), jnp.bfloat16)],
        compiler_params=pltpu.CompilerParams(vmem_limit_bytes=8 << 20),
        name="arrange",
    )(here, *parts)


def project_kernel(where_ref, n_ref, mine_ref, got_ref, *refs):
    *w_refs, own_ref, send_ref, w_all = refs
    x = where_ref[0]
    step = w_refs[0].shape[0]
    for d, w_ref in enumerate(w_refs):
        at = lax.rem(x + d, len(w_refs)) * step
        w_all[pl.ds(pl.multiple_of(at, step), step), :] = w_ref[...]
    rows = n_ref.shape[0] // 4
    for b in range(4):
        part = jnp.dot(
            n_ref[b * rows : (b + 1) * rows, :], w_all[...], preferred_element_type=jnp.float32
        )
        if b % 2 == 0:
            part = part - (mine_ref, got_ref)[b // 2][...].astype(jnp.float32)
        own_ref[b * rows : (b + 1) * rows, :] = part
        t = b ^ 1
        send_ref[t * rows : (t + 1) * rows, :] = part.astype(jnp.bfloat16)


def project(n_all, pieces, a_mine, a_got):
    here = jnp.stack([lax.axis_index("x")]).astype(jnp.int32)
    vmem = pl.BlockSpec(memory_space=pltpu.VMEM)
    shape = (n_all.shape[0], HALF)
    return pl.pallas_call(
        project_kernel,
        out_shape=(
            jax.ShapeDtypeStruct(shape, jnp.float32),
            jax.ShapeDtypeStruct(shape, jnp.bfloat16),
        ),
        in_specs=[pl.BlockSpec(memory_space=pltpu.SMEM)] + [vmem] * (3 + len(pieces)),
        out_specs=(vmem, vmem),
        scratch_shapes=[pltpu.VMEM((n_all.shape[1], HALF), jnp.bfloat16)],
        compiler_params=pltpu.CompilerParams(vmem_limit_bytes=12 << 20),
        name="project",
    )(here, n_all, a_mine, a_got, *pieces)


def halves(x, which):
    half = x.shape[1] // 2
    low, high = x[:, :half], x[:, half:]
    return jnp.where(which == 0, low, high), jnp.where(which == 0, high, low)


def partner(x, axis, mask):
    size = SIZES[AXES.index(axis)]
    return lax.ppermute(x, axis, [(i, i ^ mask) for i in range(size)])


def from_next(x, axis, distance):
    size = SIZES[AXES.index(axis)]
    return lax.ppermute(x, axis, [((i + distance) % size, i) for i in range(size)])


def local(student_in, weight, queries, keys, values, lengths, assignment):
    rows = queries.shape[0]
    core = lax.axis_index("core")
    ylo = lax.axis_index("ylo")
    wrows = weight.shape[0]

    here = jnp.stack([lax.axis_index("z"), lax.axis_index("yhi"), core]).astype(jnp.int32)
    w_mine, w_other = halves(weight, core)
    w_got = partner(w_other, "core", 1)
    kv = jnp.concatenate([keys, values], axis=1)
    pad = jnp.zeros((16 - wrows, HALF), jnp.bfloat16)
    packed = jnp.concatenate([kv, w_mine, pad, w_got, pad], axis=0)
    packed = jnp.concatenate([packed, partner(packed, "yhi", 1)], axis=0)
    up = down = packed
    held = {0: packed}
    for d in range(1, 5):
        up = from_next(up, "z", 1)
        held[d] = up
        if d < 4:
            down = from_next(down, "z", -1)
            held[-d] = down
    parts = [held[d] for d in RING]
    w_near = arrange(here, parts, wrows)
    pieces = [w_near] + [from_next(w_near, "x", d) for d in range(1, 4)]

    student_in, _ = lax.optimization_barrier((student_in, (held[1], held[-1])))
    as_float = student_in.astype(jnp.float32)
    normed = (
        as_float * lax.rsqrt(jnp.mean(as_float * as_float, axis=1, keepdims=True) + EPSILON)
    ).astype(jnp.bfloat16)
    n_keep, n_send = halves(normed, ylo)
    n_got, _ = lax.optimization_barrier((partner(n_send, "ylo", 1), w_near))
    n_pair = jnp.concatenate([n_keep, n_got], axis=0)
    n_all = jnp.concatenate([n_pair, partner(n_pair, "core", 1)], axis=0)

    parts, _ = lax.optimization_barrier((parts, w_near))
    attention, a_mine, a_other = attend(here, queries, parts, lengths, assignment)

    own, send = project(n_all, pieces, a_mine, partner(a_other, "core", 1))
    diff = own + partner(send, "ylo", 1).astype(jnp.float32)
    scaled = (diff * TOKENS_ALL ** (-0.5)).astype(jnp.bfloat16)
    part = lax.dot_general(
        n_all, scaled, (((0,), (0,)), ((), ())), preferred_element_type=jnp.float32
    ).astype(jnp.bfloat16)
    part = part.reshape(4, -1, HALF)
    x = lax.axis_index("x")
    near = lax.dynamic_index_in_dim(part, x, 0, keepdims=False).astype(jnp.float32)
    for d in range(1, 4):
        away = lax.dynamic_index_in_dim(part, (x - d) % 4, 0, keepdims=False)
        near = near + from_next(away, "x", d).astype(jnp.float32)
    near = near.astype(jnp.bfloat16).reshape(-1, wrows, HALF)
    near = jnp.pad(near, ((0, 0), (0, 16 - wrows), (0, 0)))
    last = lax.all_to_all(near, ("core", *SEQ), split_axis=0, concat_axis=0, tiled=True)
    summed = last.reshape(2, 16, 16, HALF).astype(jnp.float32).sum(axis=1)
    weight_grad = jnp.concatenate([summed[0, :wrows], summed[1, :wrows]], axis=1)
    return (attention, weight_grad)


def solution(mesh):
    mesh = Mesh(mesh.devices.reshape(SIZES), AXES)
    token = P(AXES, None)
    row = P(("ylo", "x", "core"), None)
    return jax.shard_map(
        local,
        mesh=mesh,
        in_specs=(token, token, token, token, token, row, row),
        out_specs=(token, token),
        check_vma=False,
    )
```

```python
import math

import jax
import jax.numpy as jnp
from jax import lax
from jax.experimental import pallas as pl
from jax.experimental.pallas import tpu as pltpu
from jax.sharding import Mesh, PartitionSpec as P

HD = 128
HQ = 4
BLK = 128
COLS = HQ * HD
HALF = COLS // 2
TOKENS_ALL = 32768
PADDED = 16

EPSILON = 1e-06
NEGATIVE = -1e30
LOG2E = math.log2(math.e)

AXES = ("ylo", "x", "core", "z", "yhi")
SIZES = (2, 4, 2, 8, 2)
SEQ = ("z", "yhi")

NEAR = (0, 1, -1, 2, -2)
FAR = (3, -3, 4)

SMEM = pl.BlockSpec(memory_space=pltpu.SMEM)
VMEM = pl.BlockSpec(memory_space=pltpu.VMEM)


def normalise_kernel(where_ref, student_ref, keep_ref, send_ref, spread_ref, *, wrows):
    core = where_ref[2]
    rows, features = student_ref.shape
    chunk, wide = spread_ref.shape
    target = lax.broadcasted_iota(jnp.int32, (1, wide), 1)
    inside = lax.rem(target, PADDED)
    target = jnp.where(inside < wrows, target // PADDED * wrows + inside, -1)
    source = lax.broadcasted_iota(jnp.int32, (chunk, 1), 0)
    spread_ref[...] = jnp.where(source == target, 1.0, 0.0).astype(jnp.bfloat16)
    as_float = student_ref[...].astype(jnp.float32)
    scale = lax.rsqrt(jnp.mean(as_float * as_float, axis=1, keepdims=True) + EPSILON)
    normed = (as_float * scale).astype(jnp.bfloat16)
    group = 16 * PADDED
    for k in range(features // chunk):
        apart = jnp.dot(
            normed[:, k * chunk : (k + 1) * chunk],
            spread_ref[...],
            preferred_element_type=jnp.float32,
        ).astype(jnp.bfloat16)
        for q in range(wide // group):
            g = k * (wide // group) + q
            at = (g // 2 % 4 * 2 + g // 8) * group
            piece = apart[:, q * group : (q + 1) * group]

            @pl.when(core == g % 2)
            def _():
                keep_ref[:, at : at + group] = piece

            @pl.when(core != g % 2)
            def _():
                send_ref[:, at : at + group] = piece


def normalise(here, student_in, wrows):
    rows, features = student_in.shape
    shape = jax.ShapeDtypeStruct((rows, features // wrows * PADDED // 2), jnp.bfloat16)
    chunk = features // 4

    def body(*refs):
        normalise_kernel(*refs, wrows=wrows)

    return pl.pallas_call(
        body,
        out_shape=(shape, shape),
        in_specs=[SMEM, VMEM],
        out_specs=(VMEM, VMEM),
        scratch_shapes=[pltpu.VMEM((chunk, chunk // wrows * PADDED), jnp.bfloat16)],
        compiler_params=pltpu.CompilerParams(vmem_limit_bytes=16 << 20),
        name="normalise",
    )(here, student_in)


def pack_kernel(kv_ref, kv_other_ref, *refs):
    *w_refs, out_ref = refs
    rows = kv_ref.shape[0]
    wrows, width = w_refs[0].shape
    out_ref[:rows, :] = kv_ref[...]
    out_ref[rows : 2 * rows, :] = kv_other_ref[...]
    for i, w_ref in enumerate(w_refs):
        first = 2 * rows + i * PADDED
        out_ref[first : first + PADDED, :] = jnp.concatenate(
            [w_ref[...], jnp.zeros((PADDED - wrows, width), jnp.bfloat16)], axis=0
        )


def pack(kv, kv_other, w_parts):
    rows = 2 * kv.shape[0] + len(w_parts) * PADDED
    return pl.pallas_call(
        pack_kernel,
        out_shape=jax.ShapeDtypeStruct((rows, kv.shape[1]), jnp.bfloat16),
        in_specs=[VMEM] * (2 + len(w_parts)),
        out_specs=VMEM,
        compiler_params=pltpu.CompilerParams(vmem_limit_bytes=4 << 20),
        name="pack",
    )(kv, kv_other, *w_parts)


def attend_kernel(where_ref, assign_ref, length_ref, q_ref, *refs):
    *kv_refs, out_ref, mine_ref, other_ref, s_ref = refs
    z, yhi, ylo = where_ref[0], where_ref[1], where_ref[3]
    rows = q_ref.shape[0]
    own = assign_ref[0, 2 * z + yhi] * BLK
    first = length_ref[0, 0]
    second = first + length_ref[0, 1]
    third = second + length_ref[0, 2]
    q_pos = own + lax.broadcasted_iota(jnp.int32, (rows, 1), 0)
    q_start = jnp.where(
        q_pos >= third,
        third,
        jnp.where(q_pos >= second, second, jnp.where(q_pos >= first, first, 0)),
    )
    q_all = jnp.concatenate([q_ref[:, h * HD : (h + 1) * HD] for h in range(HQ)], axis=0)
    lane = lax.broadcasted_iota(jnp.int32, (1, BLK), 1)
    chunk = 2 * BLK
    top = None
    for c, (distance, kv_ref) in enumerate(zip(NEAR + FAR, kv_refs)):
        pair = lax.rem(z + distance + 8, 8) * 2
        k_pos = [assign_ref[0, pair + yhi] * BLK + lane, assign_ref[0, pair + 1 - yhi] * BLK + lane]
        k_pos = jnp.concatenate(k_pos, axis=1)
        bias = jnp.where((k_pos >= q_start) & (k_pos <= q_pos), 0.0, NEGATIVE)
        scores = lax.dot_general(
            q_all,
            kv_ref[:chunk, :HD],
            (((1,), (1,)), ((), ())),
            preferred_element_type=jnp.float32,
        )
        scores = scores.reshape(HQ, rows, chunk) * (HD ** (-0.5) * LOG2E) + bias[None]
        scores = scores.reshape(HQ * rows, chunk)
        s_ref[:, c * chunk : (c + 1) * chunk] = scores
        best = jnp.max(scores, axis=1, keepdims=True)
        top = best if top is None else jnp.maximum(top, best)
    total = jnp.zeros((HQ * rows, 1), jnp.float32)
    mixture = jnp.zeros((HQ * rows, HD), jnp.float32)
    for c, kv_ref in enumerate(kv_refs):
        terms = jnp.exp2(s_ref[:, c * chunk : (c + 1) * chunk] - top)
        total = total + jnp.sum(terms, axis=1, keepdims=True)
        mixture = mixture + jnp.dot(
            terms.astype(jnp.bfloat16), kv_ref[:chunk, HD:], preferred_element_type=jnp.float32
        )
    result = (mixture / total).astype(jnp.bfloat16)
    for h in range(HQ):
        head = result[h * rows : (h + 1) * rows]
        out_ref[:, h * HD : (h + 1) * HD] = head
        at = h % (HQ // 2) * HD

        @pl.when(ylo == h // (HQ // 2))
        def _():
            mine_ref[:, at : at + HD] = head

        @pl.when(ylo != h // (HQ // 2))
        def _():
            other_ref[:, at : at + HD] = head


def attend(here, queries, parts, lengths, assignment):
    rows = queries.shape[0]
    half = jax.ShapeDtypeStruct((rows, HALF), jnp.bfloat16)
    return pl.pallas_call(
        attend_kernel,
        out_shape=(jax.ShapeDtypeStruct((rows, COLS), jnp.bfloat16), half, half),
        in_specs=[SMEM, SMEM, SMEM, VMEM] + [VMEM] * len(parts),
        out_specs=(VMEM, VMEM, VMEM),
        scratch_shapes=[pltpu.VMEM((HQ * rows, 16 * BLK), jnp.float32)],
        compiler_params=pltpu.CompilerParams(vmem_limit_bytes=20 << 20),
        name="attend",
    )(here, assignment, lengths, queries, *parts)


def project_kernel(where_ref, n_ref, mine_ref, got_ref, *refs):
    *w_refs, own_ref, send_ref, w_all = refs
    z, yhi, ylo, x = where_ref[0], where_ref[1], where_ref[3], where_ref[4]
    group = 16 * PADDED
    for d in range(4):
        at_x = lax.rem(x + d, 4) * 2
        for batch, w_ref in zip((NEAR, FAR), w_refs[2 * d : 2 * d + 2]):
            for k, distance in enumerate(batch):
                pair = lax.rem(z + distance + 8, 8) * 2
                for t in range(2):
                    slot = pair + (yhi if t == 0 else 1 - yhi)
                    for i in range(2):
                        side = ylo if i == 0 else 1 - ylo
                        at = (at_x + side) * group + slot * PADDED
                        first = (k * 4 + t * 2 + i) * PADDED
                        w_all[pl.ds(pl.multiple_of(at, PADDED), PADDED), :] = w_ref[
                            first : first + PADDED, :
                        ]
    rows = n_ref.shape[0] // 4
    for b in range(4):
        part = jnp.dot(
            n_ref[b * rows : (b + 1) * rows, :], w_all[...], preferred_element_type=jnp.float32
        )
        if b % 2 == 0:
            part = part - (mine_ref, got_ref)[b // 2][...].astype(jnp.float32)
        own_ref[b * rows : (b + 1) * rows, :] = part
        t = b ^ 1
        send_ref[t * rows : (t + 1) * rows, :] = part.astype(jnp.bfloat16)


def project(here, n_all, a_mine, a_got, w_parts):
    shape = (n_all.shape[0], HALF)
    return pl.pallas_call(
        project_kernel,
        out_shape=(
            jax.ShapeDtypeStruct(shape, jnp.float32),
            jax.ShapeDtypeStruct(shape, jnp.bfloat16),
        ),
        in_specs=[SMEM] + [VMEM] * (3 + len(w_parts)),
        out_specs=(VMEM, VMEM),
        scratch_shapes=[pltpu.VMEM((n_all.shape[1], HALF), jnp.bfloat16)],
        compiler_params=pltpu.CompilerParams(vmem_limit_bytes=12 << 20),
        name="project",
    )(here, n_all, a_mine, a_got, *w_parts)


def halves(x, which):
    half = x.shape[1] // 2
    low, high = x[:, :half], x[:, half:]
    return jnp.where(which == 0, low, high), jnp.where(which == 0, high, low)


def partner(x, axis):
    return lax.ppermute(x, axis, [(0, 1), (1, 0)])


def from_next(x, axis, distance):
    size = SIZES[AXES.index(axis)]
    return lax.ppermute(x, axis, [((i + distance) % size, i) for i in range(size)])


def local(student_in, weight, queries, keys, values, lengths, assignment):
    names = ("z", "yhi", "core", "ylo", "x")
    here = jnp.stack([lax.axis_index(a) for a in names]).astype(jnp.int32)
    ylo, x = here[3], here[4]
    wrows = weight.shape[0]

    kv = jnp.concatenate([keys, values], axis=1)
    kv_other = partner(kv, "yhi")
    w_mine, w_other = halves(weight, ylo)
    w_parts = [
        w_mine,
        partner(w_other, "ylo"),
        partner(w_mine, "yhi"),
        lax.ppermute(w_other, ("ylo", "yhi"), [(i, 3 - i) for i in range(4)]),
    ]

    student_in, _ = lax.optimization_barrier((student_in, (kv, w_mine)))
    n_keep, n_send = normalise(here, student_in, wrows)
    n_keep, n_send, kv_other, w_parts = lax.optimization_barrier(
        (n_keep, n_send, kv_other, w_parts)
    )
    packed = pack(kv, kv_other, w_parts)
    n_got = partner(n_send, "core")
    n_got, _ = lax.optimization_barrier((n_got, packed))
    n_pair = jnp.concatenate([n_keep, n_got], axis=0)
    n_all = jnp.concatenate([n_pair, partner(n_pair, "ylo")], axis=0)

    up = down = packed
    held = {0: packed}
    for d in range(1, 5):
        up = from_next(up, "z", 1)
        held[d] = up
        if d < 4:
            down = from_next(down, "z", -1)
            held[-d] = down
    near_rows = jnp.concatenate([held[d][2 * BLK :] for d in NEAR], axis=0)
    far_rows = jnp.concatenate([held[d][2 * BLK :] for d in FAR], axis=0)
    near_got = [from_next(near_rows, "x", d) for d in range(1, 4)]
    far_rows, near_got = lax.optimization_barrier((far_rows, near_got))
    far_got = [from_next(far_rows, "x", d) for d in range(1, 4)]
    w_all = [near_rows, far_rows]
    for pair in zip(near_got, far_got):
        w_all += pair

    parts = [held[d] for d in NEAR + FAR]
    parts, _ = lax.optimization_barrier((parts, far_rows))
    attention, a_mine, a_other = attend(here, queries, parts, lengths, assignment)

    own, send = project(here, n_all, a_mine, partner(a_other, "ylo"), w_all)
    diff = own + partner(send, "core").astype(jnp.float32)
    scaled = (diff * TOKENS_ALL ** (-0.5)).astype(jnp.bfloat16)
    part = lax.dot_general(
        n_all, scaled, (((0,), (0,)), ((), ())), preferred_element_type=jnp.float32
    ).astype(jnp.bfloat16)
    part = part.reshape(4, 32, PADDED, HALF)[:, :, :wrows].reshape(4, 32 * wrows, HALF)
    near = lax.dynamic_index_in_dim(part, x, 0, keepdims=False).astype(jnp.float32)
    for d in range(1, 4):
        away = lax.dynamic_index_in_dim(part, (x - d) % 4, 0, keepdims=False)
        near = near + from_next(away, "x", d).astype(jnp.float32)
    near = near.astype(jnp.bfloat16).reshape(-1, wrows, HALF)
    near = jnp.pad(near, ((0, 0), (0, PADDED - wrows), (0, 0)))
    last = lax.all_to_all(near, ("ylo", *SEQ), split_axis=0, concat_axis=0, tiled=True)
    summed = last.reshape(2, 16, PADDED, HALF).astype(jnp.float32).sum(axis=1)
    weight_grad = jnp.concatenate([summed[0, :wrows], summed[1, :wrows]], axis=1)
    return (attention, weight_grad)


def solution(mesh):
    mesh = Mesh(mesh.devices.reshape(SIZES), AXES)
    token = P(AXES, None)
    row = P(("ylo", "x", "core"), None)
    return jax.shard_map(
        local,
        mesh=mesh,
        in_specs=(token, token, token, token, token, row, row),
        out_specs=(token, token),
        check_vma=False,
    )
```

```python
import math

import jax
import jax.numpy as jnp
from jax import lax
from jax.experimental import pallas as pl
from jax.experimental.pallas import tpu as pltpu
from jax.sharding import Mesh, PartitionSpec as P

HD = 128
HQ = 4
BLK = 128
COLS = HQ * HD
HALF = COLS // 2
TOKENS_ALL = 32768
PADDED = 16

EPSILON = 1e-06
NEGATIVE = -1e30
LOG2E = math.log2(math.e)

AXES = ("ylo", "x", "core", "z", "yhi")
SIZES = (2, 4, 2, 8, 2)
SEQ = ("z", "yhi")

NEAR = (0, 1, -1, 2, -2)
FAR = (3, -3, 4)

SMEM = pl.BlockSpec(memory_space=pltpu.SMEM)
VMEM = pl.BlockSpec(memory_space=pltpu.VMEM)


def spread_tile(first, last, wide, wrows):
    target = lax.broadcasted_iota(jnp.int32, (1, wide), 1)
    inside = lax.rem(target, PADDED)
    target = jnp.where(inside < wrows, target // PADDED * wrows + inside, -1)
    source = lax.broadcasted_iota(jnp.int32, (last - first, 1), 0) + first
    return jnp.where(source == target, 1.0, 0.0).astype(jnp.bfloat16)


def normalise_kernel(where_ref, student_ref, keep_ref, send_ref, *, wrows):
    core = where_ref[2]
    rows, features = student_ref.shape
    group = 16 * PADDED
    taken = 16 * wrows
    chunk = features // 4
    as_float = student_ref[...].astype(jnp.float32)
    scale = lax.rsqrt(jnp.mean(as_float * as_float, axis=1, keepdims=True) + EPSILON)
    normed = (as_float * scale).astype(jnp.bfloat16)
    stacked = jnp.concatenate([normed[:, k * chunk : (k + 1) * chunk] for k in range(4)], axis=0)
    for q in range(chunk // taken):
        first = q * taken // 128 * 128
        last = min(chunk, -(-(q + 1) * taken // 128) * 128)
        tile = spread_tile(first - q * taken, last - q * taken, group, wrows)
        apart = jnp.dot(
            stacked[:, first:last], tile, preferred_element_type=jnp.float32
        ).astype(jnp.bfloat16)
        for k in range(4):
            g = k * (chunk // taken) + q
            at = (g // 2 % 4 * 2 + g // 8) * group
            piece = apart[k * rows : (k + 1) * rows]

            @pl.when(core == g % 2)
            def _():
                keep_ref[:, at : at + group] = piece

            @pl.when(core != g % 2)
            def _():
                send_ref[:, at : at + group] = piece


def normalise(here, student_in, wrows):
    rows, features = student_in.shape
    shape = jax.ShapeDtypeStruct((rows, features // wrows * PADDED // 2), jnp.bfloat16)

    def body(*refs):
        normalise_kernel(*refs, wrows=wrows)

    return pl.pallas_call(
        body,
        out_shape=(shape, shape),
        in_specs=[SMEM, VMEM],
        out_specs=(VMEM, VMEM),
        compiler_params=pltpu.CompilerParams(vmem_limit_bytes=16 << 20),
        name="normalise",
    )(here, student_in)


def pack_kernel(kv_ref, kv_other_ref, *refs):
    *w_refs, out_ref = refs
    rows = kv_ref.shape[0]
    wrows, width = w_refs[0].shape
    out_ref[:rows, :] = kv_ref[...]
    out_ref[rows : 2 * rows, :] = kv_other_ref[...]
    for i, w_ref in enumerate(w_refs):
        first = 2 * rows + i * PADDED
        out_ref[first : first + PADDED, :] = jnp.concatenate(
            [w_ref[...], jnp.zeros((PADDED - wrows, width), jnp.bfloat16)], axis=0
        )


def pack(kv, kv_other, w_parts):
    rows = 2 * kv.shape[0] + len(w_parts) * PADDED
    return pl.pallas_call(
        pack_kernel,
        out_shape=jax.ShapeDtypeStruct((rows, kv.shape[1]), jnp.bfloat16),
        in_specs=[VMEM] * (2 + len(w_parts)),
        out_specs=VMEM,
        compiler_params=pltpu.CompilerParams(vmem_limit_bytes=4 << 20),
        name="pack",
    )(kv, kv_other, *w_parts)


def attend_kernel(where_ref, assign_ref, length_ref, q_ref, *refs):
    *kv_refs, out_ref, mine_ref, other_ref, s_ref = refs
    z, yhi, ylo = where_ref[0], where_ref[1], where_ref[3]
    rows = q_ref.shape[0]
    own = assign_ref[0, 2 * z + yhi] * BLK
    first = length_ref[0, 0]
    second = first + length_ref[0, 1]
    third = second + length_ref[0, 2]
    q_pos = own + lax.broadcasted_iota(jnp.int32, (rows, 1), 0)
    q_start = jnp.where(
        q_pos >= third,
        third,
        jnp.where(q_pos >= second, second, jnp.where(q_pos >= first, first, 0)),
    )
    q_all = jnp.concatenate([q_ref[:, h * HD : (h + 1) * HD] for h in range(HQ)], axis=0)
    lane = lax.broadcasted_iota(jnp.int32, (1, BLK), 1)
    chunk = 2 * BLK
    top = None
    for c, (distance, kv_ref) in enumerate(zip(NEAR + FAR, kv_refs)):
        pair = lax.rem(z + distance + 8, 8) * 2
        k_pos = [assign_ref[0, pair + yhi] * BLK + lane, assign_ref[0, pair + 1 - yhi] * BLK + lane]
        k_pos = jnp.concatenate(k_pos, axis=1)
        bias = jnp.where((k_pos >= q_start) & (k_pos <= q_pos), 0.0, NEGATIVE)
        scores = lax.dot_general(
            q_all,
            kv_ref[:chunk, :HD],
            (((1,), (1,)), ((), ())),
            preferred_element_type=jnp.float32,
        )
        scores = scores.reshape(HQ, rows, chunk) * (HD ** (-0.5) * LOG2E) + bias[None]
        scores = scores.reshape(HQ * rows, chunk)
        s_ref[:, c * chunk : (c + 1) * chunk] = scores
        best = jnp.max(scores, axis=1, keepdims=True)
        top = best if top is None else jnp.maximum(top, best)
    total = jnp.zeros((HQ * rows, 1), jnp.float32)
    mixture = jnp.zeros((HQ * rows, HD), jnp.float32)
    for c, kv_ref in enumerate(kv_refs):
        terms = jnp.exp2(s_ref[:, c * chunk : (c + 1) * chunk] - top)
        total = total + jnp.sum(terms, axis=1, keepdims=True)
        mixture = mixture + jnp.dot(
            terms.astype(jnp.bfloat16), kv_ref[:chunk, HD:], preferred_element_type=jnp.float32
        )
    result = (mixture / total).astype(jnp.bfloat16)
    for h in range(HQ):
        head = result[h * rows : (h + 1) * rows]
        out_ref[:, h * HD : (h + 1) * HD] = head
        at = h % (HQ // 2) * HD

        @pl.when(ylo == h // (HQ // 2))
        def _():
            mine_ref[:, at : at + HD] = head

        @pl.when(ylo != h // (HQ // 2))
        def _():
            other_ref[:, at : at + HD] = head


def attend(here, queries, parts, lengths, assignment):
    rows = queries.shape[0]
    half = jax.ShapeDtypeStruct((rows, HALF), jnp.bfloat16)
    return pl.pallas_call(
        attend_kernel,
        out_shape=(jax.ShapeDtypeStruct((rows, COLS), jnp.bfloat16), half, half),
        in_specs=[SMEM, SMEM, SMEM, VMEM] + [VMEM] * len(parts),
        out_specs=(VMEM, VMEM, VMEM),
        scratch_shapes=[pltpu.VMEM((HQ * rows, 16 * BLK), jnp.float32)],
        compiler_params=pltpu.CompilerParams(vmem_limit_bytes=20 << 20),
        name="attend",
    )(here, assignment, lengths, queries, *parts)


def project_kernel(where_ref, n_ref, mine_ref, got_ref, *refs):
    *w_refs, own_ref, send_ref, w_all = refs
    z, yhi, ylo, x = where_ref[0], where_ref[1], where_ref[3], where_ref[4]
    group = 16 * PADDED
    for d in range(4):
        at_x = lax.rem(x + d, 4) * 2
        for batch, w_ref in zip((NEAR, FAR), w_refs[2 * d : 2 * d + 2]):
            for k, distance in enumerate(batch):
                pair = lax.rem(z + distance + 8, 8) * 2
                for t in range(2):
                    slot = pair + (yhi if t == 0 else 1 - yhi)
                    for i in range(2):
                        side = ylo if i == 0 else 1 - ylo
                        at = (at_x + side) * group + slot * PADDED
                        first = (k * 4 + t * 2 + i) * PADDED
                        w_all[pl.ds(pl.multiple_of(at, PADDED), PADDED), :] = w_ref[
                            first : first + PADDED, :
                        ]
    rows = n_ref.shape[0] // 4
    for b in range(4):
        part = jnp.dot(
            n_ref[b * rows : (b + 1) * rows, :], w_all[...], preferred_element_type=jnp.float32
        )
        if b % 2 == 0:
            part = part - (mine_ref, got_ref)[b // 2][...].astype(jnp.float32)
        own_ref[b * rows : (b + 1) * rows, :] = part
        t = b ^ 1
        send_ref[t * rows : (t + 1) * rows, :] = part.astype(jnp.bfloat16)


def project(here, n_all, a_mine, a_got, w_parts):
    shape = (n_all.shape[0], HALF)
    return pl.pallas_call(
        project_kernel,
        out_shape=(
            jax.ShapeDtypeStruct(shape, jnp.float32),
            jax.ShapeDtypeStruct(shape, jnp.bfloat16),
        ),
        in_specs=[SMEM] + [VMEM] * (3 + len(w_parts)),
        out_specs=(VMEM, VMEM),
        scratch_shapes=[pltpu.VMEM((n_all.shape[1], HALF), jnp.bfloat16)],
        compiler_params=pltpu.CompilerParams(vmem_limit_bytes=12 << 20),
        name="project",
    )(here, n_all, a_mine, a_got, *w_parts)


def halves(x, which):
    half = x.shape[1] // 2
    low, high = x[:, :half], x[:, half:]
    return jnp.where(which == 0, low, high), jnp.where(which == 0, high, low)


def gradient_kernel(where_ref, n_ref, own_ref, back_ref, *out_refs):
    x = where_ref[4]
    columns = n_ref.shape[1] // 4
    taken = out_refs[0].shape[0]
    wrows = taken * PADDED // columns
    diff = own_ref[...] + back_ref[...].astype(jnp.float32)
    scaled = (diff * TOKENS_ALL ** (-0.5)).astype(jnp.bfloat16)
    step = 128 // PADDED * wrows
    target = lax.broadcasted_iota(jnp.int32, (1, 128), 1)
    inside = lax.rem(target, PADDED)
    target = jnp.where(inside < wrows, target // PADDED * wrows + inside, -1)
    row = lax.broadcasted_iota(jnp.int32, (step, 1), 0)
    cut = jnp.where(row == target, 1.0, 0.0).astype(jnp.bfloat16)
    for d, out_ref in enumerate(out_refs):
        at = pl.multiple_of(lax.rem(x + 4 - d, 4) * columns, columns)
        part = lax.dot_general(
            n_ref[:, pl.ds(at, columns)],
            scaled,
            (((0,), (0,)), ((), ())),
            preferred_element_type=jnp.float32,
        ).astype(jnp.bfloat16)
        for j in range(columns // 128):
            out_ref[j * step : (j + 1) * step, :] = jnp.dot(
                cut, part[j * 128 : (j + 1) * 128], preferred_element_type=jnp.float32
            ).astype(jnp.bfloat16)


def gradient(here, n_all, own, back, wrows):
    shape = jax.ShapeDtypeStruct((n_all.shape[1] // 4 // PADDED * wrows, HALF), jnp.bfloat16)
    return pl.pallas_call(
        gradient_kernel,
        out_shape=(shape,) * 4,
        in_specs=[SMEM, VMEM, VMEM, VMEM],
        out_specs=(VMEM,) * 4,
        compiler_params=pltpu.CompilerParams(vmem_limit_bytes=16 << 20),
        name="gradient",
    )(here, n_all, own, back)


def partner(x, axis):
    return lax.ppermute(x, axis, [(0, 1), (1, 0)])


def from_next(x, axis, distance):
    size = SIZES[AXES.index(axis)]
    return lax.ppermute(x, axis, [((i + distance) % size, i) for i in range(size)])


def local(student_in, weight, queries, keys, values, lengths, assignment):
    names = ("z", "yhi", "core", "ylo", "x")
    here = jnp.stack([lax.axis_index(a) for a in names]).astype(jnp.int32)
    wrows = weight.shape[0]

    lane = lax.broadcasted_iota(jnp.int32, (keys.shape[0], 2 * HD), 1)
    kv = jnp.where(
        lane < HD, jnp.pad(keys, ((0, 0), (0, HD))), jnp.pad(values, ((0, 0), (HD, 0)))
    )
    w_mine, w_other = halves(weight, here[3])
    kv_other = partner(kv, "yhi")
    w_parts = [
        w_mine,
        partner(w_other, "ylo"),
        partner(w_mine, "yhi"),
        lax.ppermute(w_other, ("ylo", "yhi"), [(i, 3 - i) for i in range(4)]),
    ]
    packed = pack(kv, kv_other, w_parts)

    student_in, _ = lax.optimization_barrier((student_in, packed))
    n_keep, n_send = normalise(here, student_in, wrows)
    up, down = from_next(packed, "z", 1), from_next(packed, "z", -1)
    up, down, n_keep, n_send = lax.optimization_barrier((up, down, n_keep, n_send))
    n_pair = jnp.concatenate([n_keep, partner(n_send, "core")], axis=0)
    n_all = jnp.concatenate([n_pair, partner(n_pair, "ylo")], axis=0)

    held = {0: packed, 1: up, -1: down}
    for d in range(2, 5):
        held[d] = from_next(held[d - 1], "z", 1)
        if d < 4:
            held[-d] = from_next(held[1 - d], "z", -1)
    near_rows = jnp.concatenate([held[d][2 * BLK :] for d in NEAR], axis=0)
    far_rows = jnp.concatenate([held[d][2 * BLK :] for d in FAR], axis=0)
    near_got = [from_next(near_rows, "x", d) for d in range(1, 4)]
    far_rows, near_got = lax.optimization_barrier((far_rows, near_got))
    far_got = [from_next(far_rows, "x", d) for d in range(1, 4)]
    w_all = [near_rows, far_rows]
    for pair in zip(near_got, far_got):
        w_all += pair

    parts = [held[d] for d in NEAR + FAR]
    parts, _ = lax.optimization_barrier((parts, far_rows))
    attention, a_mine, a_other = attend(here, queries, parts, lengths, assignment)

    own, send = project(here, n_all, a_mine, partner(a_other, "ylo"), w_all)
    near, *away = gradient(here, n_all, own, partner(send, "core"), wrows)
    near = near.astype(jnp.float32)
    for d in range(1, 4):
        near = near + from_next(away[d - 1], "x", d).astype(jnp.float32)
    near = near.astype(jnp.bfloat16).reshape(-1, wrows, HALF)
    near = jnp.pad(near, ((0, 0), (0, PADDED - wrows), (0, 0)))
    last = lax.all_to_all(near, ("ylo", *SEQ), split_axis=0, concat_axis=0, tiled=True)
    summed = last.reshape(2, 16, PADDED, HALF).astype(jnp.float32).sum(axis=1)
    weight_grad = jnp.concatenate([summed[0, :wrows], summed[1, :wrows]], axis=1)
    return (attention, weight_grad)


def solution(mesh):
    mesh = Mesh(mesh.devices.reshape(SIZES), AXES)
    token = P(AXES, None)
    row = P(("ylo", "x", "core"), None)
    return jax.shard_map(
        local,
        mesh=mesh,
        in_specs=(token, token, token, token, token, row, row),
        out_specs=(token, token),
        check_vma=False,
    )
```

```python
import math

import jax
import jax.numpy as jnp
from jax import lax
from jax.experimental import pallas as pl
from jax.experimental.pallas import tpu as pltpu
from jax.sharding import Mesh, PartitionSpec as P

HD = 128
HQ = 4
BLK = 128
COLS = HQ * HD
HALF = COLS // 2
TOKENS_ALL = 32768
PADDED = 16

EPSILON = 1e-06
NEGATIVE = -1e30
LOG2E = math.log2(math.e)

AXES = ("ylo", "x", "core", "z", "yhi")
SIZES = (2, 4, 2, 8, 2)
SEQ = ("z", "yhi")

RING = (0, 1, -1, 2, -2, 3, -3, 4)

SMEM = pl.BlockSpec(memory_space=pltpu.SMEM)
VMEM = pl.BlockSpec(memory_space=pltpu.VMEM)


def spread_tile(first, last, wide, wrows):
    target = lax.broadcasted_iota(jnp.int32, (1, wide), 1)
    inside = lax.rem(target, PADDED)
    target = jnp.where(inside < wrows, target // PADDED * wrows + inside, -1)
    source = lax.broadcasted_iota(jnp.int32, (last - first, 1), 0) + first
    return jnp.where(source == target, 1.0, 0.0).astype(jnp.bfloat16)


def normalise_kernel(where_ref, student_ref, keep_ref, send_ref, *, wrows):
    core = where_ref[2]
    rows, features = student_ref.shape
    group = 16 * PADDED
    taken = 16 * wrows
    chunk = features // 4
    as_float = student_ref[...].astype(jnp.float32)
    scale = lax.rsqrt(jnp.mean(as_float * as_float, axis=1, keepdims=True) + EPSILON)
    normed = (as_float * scale).astype(jnp.bfloat16)
    stacked = jnp.concatenate([normed[:, k * chunk : (k + 1) * chunk] for k in range(4)], axis=0)
    for q in range(chunk // taken):
        first = q * taken // 128 * 128
        last = min(chunk, -(-(q + 1) * taken // 128) * 128)
        tile = spread_tile(first - q * taken, last - q * taken, group, wrows)
        apart = jnp.dot(
            stacked[:, first:last], tile, preferred_element_type=jnp.float32
        ).astype(jnp.bfloat16)
        for k in range(4):
            g = k * (chunk // taken) + q
            at = (g // 2 % 4 * 2 + g // 8) * group
            piece = apart[k * rows : (k + 1) * rows]

            @pl.when(core == g % 2)
            def _():
                keep_ref[:, at : at + group] = piece

            @pl.when(core != g % 2)
            def _():
                send_ref[:, at : at + group] = piece


def normalise(here, student_in, wrows):
    rows, features = student_in.shape
    shape = jax.ShapeDtypeStruct((rows, features // wrows * PADDED // 2), jnp.bfloat16)

    def body(*refs):
        normalise_kernel(*refs, wrows=wrows)

    return pl.pallas_call(
        body,
        out_shape=(shape, shape),
        in_specs=[SMEM, VMEM],
        out_specs=(VMEM, VMEM),
        compiler_params=pltpu.CompilerParams(vmem_limit_bytes=16 << 20),
        name="normalise",
    )(here, student_in)


def pack_kernel(kv_ref, kv_other_ref, *refs):
    *w_refs, out_ref = refs
    rows = kv_ref.shape[0]
    wrows, width = w_refs[0].shape
    out_ref[:rows, :] = kv_ref[...]
    out_ref[rows : 2 * rows, :] = kv_other_ref[...]
    for i, w_ref in enumerate(w_refs):
        first = 2 * rows + i * PADDED
        out_ref[first : first + PADDED, :] = jnp.concatenate(
            [w_ref[...], jnp.zeros((PADDED - wrows, width), jnp.bfloat16)], axis=0
        )


def pack(kv, kv_other, w_parts):
    rows = 2 * kv.shape[0] + len(w_parts) * PADDED
    return pl.pallas_call(
        pack_kernel,
        out_shape=jax.ShapeDtypeStruct((rows, kv.shape[1]), jnp.bfloat16),
        in_specs=[VMEM] * (2 + len(w_parts)),
        out_specs=VMEM,
        compiler_params=pltpu.CompilerParams(vmem_limit_bytes=4 << 20),
        name="pack",
    )(kv, kv_other, *w_parts)


def attend_kernel(where_ref, assign_ref, length_ref, q_ref, *refs):
    *kv_refs, out_ref, mine_ref, other_ref, s_ref = refs
    z, yhi, ylo = where_ref[0], where_ref[1], where_ref[3]
    rows = q_ref.shape[0]
    own = assign_ref[0, 2 * z + yhi] * BLK
    first = length_ref[0, 0]
    second = first + length_ref[0, 1]
    third = second + length_ref[0, 2]
    q_pos = own + lax.broadcasted_iota(jnp.int32, (rows, 1), 0)
    q_start = jnp.where(
        q_pos >= third,
        third,
        jnp.where(q_pos >= second, second, jnp.where(q_pos >= first, first, 0)),
    )
    q_all = jnp.concatenate([q_ref[:, h * HD : (h + 1) * HD] for h in range(HQ)], axis=0)
    lane = lax.broadcasted_iota(jnp.int32, (1, BLK), 1)
    chunk = 2 * BLK
    top = None
    for c, (distance, kv_ref) in enumerate(zip(RING, kv_refs)):
        pair = lax.rem(z + distance + 8, 8) * 2
        k_pos = [assign_ref[0, pair + yhi] * BLK + lane, assign_ref[0, pair + 1 - yhi] * BLK + lane]
        k_pos = jnp.concatenate(k_pos, axis=1)
        bias = jnp.where((k_pos >= q_start) & (k_pos <= q_pos), 0.0, NEGATIVE)
        scores = lax.dot_general(
            q_all,
            kv_ref[:chunk, :HD],
            (((1,), (1,)), ((), ())),
            preferred_element_type=jnp.float32,
        )
        scores = scores.reshape(HQ, rows, chunk) * (HD ** (-0.5) * LOG2E) + bias[None]
        scores = scores.reshape(HQ * rows, chunk)
        s_ref[:, c * chunk : (c + 1) * chunk] = scores
        best = jnp.max(scores, axis=1, keepdims=True)
        top = best if top is None else jnp.maximum(top, best)
    total = jnp.zeros((HQ * rows, 1), jnp.float32)
    mixture = jnp.zeros((HQ * rows, HD), jnp.float32)
    for c, kv_ref in enumerate(kv_refs):
        terms = jnp.exp2(s_ref[:, c * chunk : (c + 1) * chunk] - top)
        total = total + jnp.sum(terms, axis=1, keepdims=True)
        mixture = mixture + jnp.dot(
            terms.astype(jnp.bfloat16), kv_ref[:chunk, HD:], preferred_element_type=jnp.float32
        )
    result = (mixture / total).astype(jnp.bfloat16)
    for h in range(HQ):
        head = result[h * rows : (h + 1) * rows]
        out_ref[:, h * HD : (h + 1) * HD] = head
        at = h % (HQ // 2) * HD

        @pl.when(ylo == h // (HQ // 2))
        def _():
            mine_ref[:, at : at + HD] = head

        @pl.when(ylo != h // (HQ // 2))
        def _():
            other_ref[:, at : at + HD] = head


def attend(here, queries, parts, lengths, assignment):
    rows = queries.shape[0]
    half = jax.ShapeDtypeStruct((rows, HALF), jnp.bfloat16)
    return pl.pallas_call(
        attend_kernel,
        out_shape=(jax.ShapeDtypeStruct((rows, COLS), jnp.bfloat16), half, half),
        in_specs=[SMEM, SMEM, SMEM, VMEM] + [VMEM] * len(parts),
        out_specs=(VMEM, VMEM, VMEM),
        scratch_shapes=[pltpu.VMEM((HQ * rows, 16 * BLK), jnp.float32)],
        compiler_params=pltpu.CompilerParams(vmem_limit_bytes=20 << 20),
        name="attend",
    )(here, assignment, lengths, queries, *parts)


def project_kernel(where_ref, n_ref, mine_ref, got_ref, *refs):
    *w_refs, own_ref, send_ref, w_all = refs
    z, yhi, ylo, x = where_ref[0], where_ref[1], where_ref[3], where_ref[4]
    group = 16 * PADDED
    for d in range(4):
        at_x = lax.rem(x + d, 4) * 2
        for k, distance in enumerate(RING):
            pair = lax.rem(z + distance + 8, 8) * 2
            for t in range(2):
                slot = pair + (yhi if t == 0 else 1 - yhi)
                for i in range(2):
                    side = ylo if i == 0 else 1 - ylo
                    at = (at_x + side) * group + slot * PADDED
                    first = (k * 4 + t * 2 + i) * PADDED
                    w_all[pl.ds(pl.multiple_of(at, PADDED), PADDED), :] = w_refs[d][
                        first : first + PADDED, :
                    ]
    rows = n_ref.shape[0] // 4
    for b in range(4):
        part = jnp.dot(
            n_ref[b * rows : (b + 1) * rows, :], w_all[...], preferred_element_type=jnp.float32
        )
        if b % 2 == 0:
            part = part - (mine_ref, got_ref)[b // 2][...].astype(jnp.float32)
        own_ref[b * rows : (b + 1) * rows, :] = part
        t = b ^ 1
        send_ref[t * rows : (t + 1) * rows, :] = part.astype(jnp.bfloat16)


def project(here, n_all, a_mine, a_got, w_parts):
    shape = (n_all.shape[0], HALF)
    return pl.pallas_call(
        project_kernel,
        out_shape=(
            jax.ShapeDtypeStruct(shape, jnp.float32),
            jax.ShapeDtypeStruct(shape, jnp.bfloat16),
        ),
        in_specs=[SMEM] + [VMEM] * (3 + len(w_parts)),
        out_specs=(VMEM, VMEM),
        scratch_shapes=[pltpu.VMEM((n_all.shape[1], HALF), jnp.bfloat16)],
        compiler_params=pltpu.CompilerParams(vmem_limit_bytes=12 << 20),
        name="project",
    )(here, n_all, a_mine, a_got, *w_parts)


def halves(x, which):
    half = x.shape[1] // 2
    low, high = x[:, :half], x[:, half:]
    return jnp.where(which == 0, low, high), jnp.where(which == 0, high, low)


def gradient_kernel(where_ref, n_ref, own_ref, back_ref, *out_refs):
    x = where_ref[4]
    columns = n_ref.shape[1] // 4
    taken = out_refs[0].shape[0]
    wrows = taken * PADDED // columns
    diff = own_ref[...] + back_ref[...].astype(jnp.float32)
    scaled = (diff * TOKENS_ALL ** (-0.5)).astype(jnp.bfloat16)
    step = 128 // PADDED * wrows
    target = lax.broadcasted_iota(jnp.int32, (1, 128), 1)
    inside = lax.rem(target, PADDED)
    target = jnp.where(inside < wrows, target // PADDED * wrows + inside, -1)
    row = lax.broadcasted_iota(jnp.int32, (step, 1), 0)
    cut = jnp.where(row == target, 1.0, 0.0).astype(jnp.bfloat16)
    for d, out_ref in enumerate(out_refs):
        at = pl.multiple_of(lax.rem(x + 4 - d, 4) * columns, columns)
        part = lax.dot_general(
            n_ref[:, pl.ds(at, columns)],
            scaled,
            (((0,), (0,)), ((), ())),
            preferred_element_type=jnp.float32,
        ).astype(jnp.bfloat16)
        for j in range(columns // 128):
            out_ref[j * step : (j + 1) * step, :] = jnp.dot(
                cut, part[j * 128 : (j + 1) * 128], preferred_element_type=jnp.float32
            ).astype(jnp.bfloat16)


def gradient(here, n_all, own, back, wrows):
    shape = jax.ShapeDtypeStruct((n_all.shape[1] // 4 // PADDED * wrows, HALF), jnp.bfloat16)
    return pl.pallas_call(
        gradient_kernel,
        out_shape=(shape,) * 4,
        in_specs=[SMEM, VMEM, VMEM, VMEM],
        out_specs=(VMEM,) * 4,
        compiler_params=pltpu.CompilerParams(vmem_limit_bytes=16 << 20),
        name="gradient",
    )(here, n_all, own, back)


def partner(x, axis):
    return lax.ppermute(x, axis, [(0, 1), (1, 0)])


def from_next(x, axis, distance):
    size = SIZES[AXES.index(axis)]
    return lax.ppermute(x, axis, [((i + distance) % size, i) for i in range(size)])


def local(student_in, weight, queries, keys, values, lengths, assignment):
    names = ("z", "yhi", "core", "ylo", "x")
    here = jnp.stack([lax.axis_index(a) for a in names]).astype(jnp.int32)
    wrows = weight.shape[0]

    lane = lax.broadcasted_iota(jnp.int32, (keys.shape[0], 2 * HD), 1)
    kv = jnp.where(
        lane < HD, jnp.pad(keys, ((0, 0), (0, HD))), jnp.pad(values, ((0, 0), (HD, 0)))
    )
    w_mine, w_other = halves(weight, here[3])
    kv_other = partner(kv, "yhi")
    w_parts = [
        w_mine,
        partner(w_other, "ylo"),
        partner(w_mine, "yhi"),
        lax.ppermute(w_other, ("ylo", "yhi"), [(i, 3 - i) for i in range(4)]),
    ]
    packed = pack(kv, kv_other, w_parts)

    student_in, _ = lax.optimization_barrier((student_in, packed))
    n_keep, n_send = normalise(here, student_in, wrows)
    up, down = from_next(packed, "z", 1), from_next(packed, "z", -1)
    up, down, n_keep, n_send = lax.optimization_barrier((up, down, n_keep, n_send))
    n_pair = jnp.concatenate([n_keep, partner(n_send, "core")], axis=0)
    held = {0: packed, 1: up, -1: down}
    for d in range(2, 5):
        held[d] = from_next(held[d - 1], "z", 1)
        if d < 4:
            held[-d] = from_next(held[1 - d], "z", -1)
        if d == 2:
            held[2], held[-2], n_pair = lax.optimization_barrier((held[2], held[-2], n_pair))
    n_all = jnp.concatenate([n_pair, partner(n_pair, "ylo")], axis=0)
    parts = [held[d] for d in RING]
    w_rows = jnp.concatenate([part[2 * BLK :] for part in parts], axis=0)
    w_all = [w_rows] + [from_next(w_rows, "x", d) for d in range(1, 4)]

    parts, _ = lax.optimization_barrier((parts, w_rows))
    attention, a_mine, a_other = attend(here, queries, parts, lengths, assignment)

    own, send = project(here, n_all, a_mine, partner(a_other, "ylo"), w_all)
    near, *away = gradient(here, n_all, own, partner(send, "core"), wrows)
    near = near.astype(jnp.float32)
    for d in range(1, 4):
        near = near + from_next(away[d - 1], "x", d).astype(jnp.float32)
    near = near.astype(jnp.bfloat16).reshape(-1, wrows, HALF)
    near = jnp.pad(near, ((0, 0), (0, PADDED - wrows), (0, 0)))
    last = lax.all_to_all(near, ("ylo", *SEQ), split_axis=0, concat_axis=0, tiled=True)
    summed = last.reshape(2, 16, PADDED, HALF).astype(jnp.float32).sum(axis=1)
    weight_grad = jnp.concatenate([summed[0, :wrows], summed[1, :wrows]], axis=1)
    return (attention, weight_grad)


def solution(mesh):
    mesh = Mesh(mesh.devices.reshape(SIZES), AXES)
    token = P(AXES, None)
    row = P(("ylo", "x", "core"), None)
    return jax.shard_map(
        local,
        mesh=mesh,
        in_specs=(token, token, token, token, token, row, row),
        out_specs=(token, token),
        check_vma=False,
    )
```

```python
import math

import jax
import jax.numpy as jnp
from jax import lax
from jax.experimental import pallas as pl
from jax.experimental.pallas import tpu as pltpu
from jax.sharding import Mesh, PartitionSpec as P

HD = 128
HQ = 4
BLK = 128
COLS = HQ * HD
HALF = COLS // 2
TOKENS_ALL = 32768
PADDED = 16

EPSILON = 1e-06
NEGATIVE = -1e30
LOG2E = math.log2(math.e)

AXES = ("ylo", "x", "core", "z", "yhi")
SIZES = (2, 4, 2, 8, 2)
SEQ = ("z", "yhi")

RING = (0, 1, -1, 2, -2, 3, -3, 4)

SMEM = pl.BlockSpec(memory_space=pltpu.SMEM)
VMEM = pl.BlockSpec(memory_space=pltpu.VMEM)


def spread_tile(first, last, wide, wrows):
    target = lax.broadcasted_iota(jnp.int32, (1, wide), 1)
    inside = lax.rem(target, PADDED)
    target = jnp.where(inside < wrows, target // PADDED * wrows + inside, -1)
    source = lax.broadcasted_iota(jnp.int32, (last - first, 1), 0) + first
    return jnp.where(source == target, 1.0, 0.0).astype(jnp.bfloat16)


def normalise_kernel(where_ref, student_ref, keep_ref, send_ref, *, wrows):
    core = where_ref[2]
    rows, features = student_ref.shape
    group = 16 * PADDED
    taken = 16 * wrows
    chunk = features // 4
    as_float = student_ref[...].astype(jnp.float32)
    scale = lax.rsqrt(jnp.mean(as_float * as_float, axis=1, keepdims=True) + EPSILON)
    normed = (as_float * scale).astype(jnp.bfloat16)
    stacked = jnp.concatenate([normed[:, k * chunk : (k + 1) * chunk] for k in range(4)], axis=0)
    for q in range(chunk // taken):
        first = q * taken // 128 * 128
        last = min(chunk, -(-(q + 1) * taken // 128) * 128)
        tile = spread_tile(first - q * taken, last - q * taken, group, wrows)
        apart = jnp.dot(
            stacked[:, first:last], tile, preferred_element_type=jnp.float32
        ).astype(jnp.bfloat16)
        for k in range(4):
            g = k * (chunk // taken) + q
            at = (g // 2 % 4 * 2 + g // 8) * group
            piece = apart[k * rows : (k + 1) * rows]

            @pl.when(core == g % 2)
            def _():
                keep_ref[:, at : at + group] = piece

            @pl.when(core != g % 2)
            def _():
                send_ref[:, at : at + group] = piece


def normalise(here, student_in, wrows):
    rows, features = student_in.shape
    shape = jax.ShapeDtypeStruct((rows, features // wrows * PADDED // 2), jnp.bfloat16)

    def body(*refs):
        normalise_kernel(*refs, wrows=wrows)

    return pl.pallas_call(
        body,
        out_shape=(shape, shape),
        in_specs=[SMEM, VMEM],
        out_specs=(VMEM, VMEM),
        compiler_params=pltpu.CompilerParams(vmem_limit_bytes=16 << 20),
        name="normalise",
    )(here, student_in)


def pack_kernel(kv_ref, kv_other_ref, *refs):
    *w_refs, out_ref = refs
    rows = kv_ref.shape[0]
    wrows, width = w_refs[0].shape
    out_ref[:rows, :] = kv_ref[...]
    out_ref[rows : 2 * rows, :] = kv_other_ref[...]
    for i, w_ref in enumerate(w_refs):
        first = 2 * rows + i * PADDED
        out_ref[first : first + PADDED, :] = jnp.concatenate(
            [w_ref[...], jnp.zeros((PADDED - wrows, width), jnp.bfloat16)], axis=0
        )


def pack(kv, kv_other, w_parts):
    rows = 2 * kv.shape[0] + len(w_parts) * PADDED
    return pl.pallas_call(
        pack_kernel,
        out_shape=jax.ShapeDtypeStruct((rows, kv.shape[1]), jnp.bfloat16),
        in_specs=[VMEM] * (2 + len(w_parts)),
        out_specs=VMEM,
        compiler_params=pltpu.CompilerParams(vmem_limit_bytes=4 << 20),
        name="pack",
    )(kv, kv_other, *w_parts)


def attend_kernel(where_ref, assign_ref, length_ref, q_ref, *refs):
    *kv_refs, out_ref, mine_ref, other_ref, s_ref = refs
    z, yhi, ylo = where_ref[0], where_ref[1], where_ref[3]
    rows = q_ref.shape[0]
    own = assign_ref[0, 2 * z + yhi] * BLK
    first = length_ref[0, 0]
    second = first + length_ref[0, 1]
    third = second + length_ref[0, 2]
    q_pos = own + lax.broadcasted_iota(jnp.int32, (rows, 1), 0)
    q_start = jnp.where(
        q_pos >= third,
        third,
        jnp.where(q_pos >= second, second, jnp.where(q_pos >= first, first, 0)),
    )
    q_all = jnp.concatenate([q_ref[:, h * HD : (h + 1) * HD] for h in range(HQ)], axis=0)
    lane = lax.broadcasted_iota(jnp.int32, (1, BLK), 1)
    chunk = 2 * BLK
    top = None
    for c, (distance, kv_ref) in enumerate(zip(RING, kv_refs)):
        pair = lax.rem(z + distance + 8, 8) * 2
        k_pos = [assign_ref[0, pair + yhi] * BLK + lane, assign_ref[0, pair + 1 - yhi] * BLK + lane]
        k_pos = jnp.concatenate(k_pos, axis=1)
        bias = jnp.where((k_pos >= q_start) & (k_pos <= q_pos), 0.0, NEGATIVE)
        scores = lax.dot_general(
            q_all,
            kv_ref[:chunk, :HD],
            (((1,), (1,)), ((), ())),
            preferred_element_type=jnp.float32,
        )
        scores = scores.reshape(HQ, rows, chunk) * (HD ** (-0.5) * LOG2E) + bias[None]
        scores = scores.reshape(HQ * rows, chunk)
        s_ref[:, c * chunk : (c + 1) * chunk] = scores
        best = jnp.max(scores, axis=1, keepdims=True)
        top = best if top is None else jnp.maximum(top, best)
    total = jnp.zeros((HQ * rows, 1), jnp.float32)
    mixture = jnp.zeros((HQ * rows, HD), jnp.float32)
    for c, kv_ref in enumerate(kv_refs):
        terms = jnp.exp2(s_ref[:, c * chunk : (c + 1) * chunk] - top)
        total = total + jnp.sum(terms, axis=1, keepdims=True)
        mixture = mixture + jnp.dot(
            terms.astype(jnp.bfloat16), kv_ref[:chunk, HD:], preferred_element_type=jnp.float32
        )
    result = (mixture / total).astype(jnp.bfloat16)
    for h in range(HQ):
        head = result[h * rows : (h + 1) * rows]
        out_ref[:, h * HD : (h + 1) * HD] = head
        at = h % (HQ // 2) * HD

        @pl.when(ylo == h // (HQ // 2))
        def _():
            mine_ref[:, at : at + HD] = head

        @pl.when(ylo != h // (HQ // 2))
        def _():
            other_ref[:, at : at + HD] = head


def attend(here, queries, parts, lengths, assignment):
    rows = queries.shape[0]
    half = jax.ShapeDtypeStruct((rows, HALF), jnp.bfloat16)
    return pl.pallas_call(
        attend_kernel,
        out_shape=(jax.ShapeDtypeStruct((rows, COLS), jnp.bfloat16), half, half),
        in_specs=[SMEM, SMEM, SMEM, VMEM] + [VMEM] * len(parts),
        out_specs=(VMEM, VMEM, VMEM),
        scratch_shapes=[pltpu.VMEM((HQ * rows, 16 * BLK), jnp.float32)],
        compiler_params=pltpu.CompilerParams(vmem_limit_bytes=20 << 20),
        name="attend",
    )(here, assignment, lengths, queries, *parts)


def project_kernel(where_ref, n_ref, mine_ref, got_ref, *refs):
    *w_refs, own_ref, send_ref, w_all = refs
    z, yhi, ylo, x = where_ref[0], where_ref[1], where_ref[3], where_ref[4]
    group = 16 * PADDED
    for d in range(4):
        at_x = lax.rem(x + d, 4) * 2
        for k, distance in enumerate(RING):
            pair = lax.rem(z + distance + 8, 8) * 2
            for t in range(2):
                slot = pair + (yhi if t == 0 else 1 - yhi)
                for i in range(2):
                    side = ylo if i == 0 else 1 - ylo
                    at = (at_x + side) * group + slot * PADDED
                    first = (k * 4 + t * 2 + i) * PADDED
                    w_all[pl.ds(pl.multiple_of(at, PADDED), PADDED), :] = w_refs[d][
                        first : first + PADDED, :
                    ]
    rows = n_ref.shape[0] // 4
    for b in range(4):
        part = jnp.dot(
            n_ref[b * rows : (b + 1) * rows, :], w_all[...], preferred_element_type=jnp.float32
        )
        if b % 2 == 0:
            part = part - (mine_ref, got_ref)[b // 2][...].astype(jnp.float32)
        own_ref[b * rows : (b + 1) * rows, :] = part
        t = b ^ 1
        send_ref[t * rows : (t + 1) * rows, :] = part.astype(jnp.bfloat16)


def project(here, n_all, a_mine, a_got, w_parts):
    shape = (n_all.shape[0], HALF)
    return pl.pallas_call(
        project_kernel,
        out_shape=(
            jax.ShapeDtypeStruct(shape, jnp.float32),
            jax.ShapeDtypeStruct(shape, jnp.bfloat16),
        ),
        in_specs=[SMEM] + [VMEM] * (3 + len(w_parts)),
        out_specs=(VMEM, VMEM),
        scratch_shapes=[pltpu.VMEM((n_all.shape[1], HALF), jnp.bfloat16)],
        compiler_params=pltpu.CompilerParams(vmem_limit_bytes=12 << 20),
        name="project",
    )(here, n_all, a_mine, a_got, *w_parts)


def halves(x, which):
    half = x.shape[1] // 2
    low, high = x[:, :half], x[:, half:]
    return jnp.where(which == 0, low, high), jnp.where(which == 0, high, low)


def gradient_kernel(where_ref, n_ref, own_ref, back_ref, *out_refs):
    x = where_ref[4]
    columns = n_ref.shape[1] // 4
    taken = out_refs[0].shape[0]
    wrows = taken * PADDED // columns
    diff = own_ref[...] + back_ref[...].astype(jnp.float32)
    scaled = (diff * TOKENS_ALL ** (-0.5)).astype(jnp.bfloat16)
    step = 128 // PADDED * wrows
    target = lax.broadcasted_iota(jnp.int32, (1, 128), 1)
    inside = lax.rem(target, PADDED)
    target = jnp.where(inside < wrows, target // PADDED * wrows + inside, -1)
    row = lax.broadcasted_iota(jnp.int32, (step, 1), 0)
    cut = jnp.where(row == target, 1.0, 0.0).astype(jnp.bfloat16)
    for d, out_ref in enumerate(out_refs):
        at = pl.multiple_of(lax.rem(x + 4 - d, 4) * columns, columns)
        part = lax.dot_general(
            n_ref[:, pl.ds(at, columns)],
            scaled,
            (((0,), (0,)), ((), ())),
            preferred_element_type=jnp.float32,
        ).astype(jnp.bfloat16)
        for j in range(columns // 128):
            out_ref[j * step : (j + 1) * step, :] = jnp.dot(
                cut, part[j * 128 : (j + 1) * 128], preferred_element_type=jnp.float32
            ).astype(jnp.bfloat16)


def gradient(here, n_all, own, back, wrows):
    shape = jax.ShapeDtypeStruct((n_all.shape[1] // 4 // PADDED * wrows, HALF), jnp.bfloat16)
    return pl.pallas_call(
        gradient_kernel,
        out_shape=(shape,) * 4,
        in_specs=[SMEM, VMEM, VMEM, VMEM],
        out_specs=(VMEM,) * 4,
        compiler_params=pltpu.CompilerParams(vmem_limit_bytes=16 << 20),
        name="gradient",
    )(here, n_all, own, back)


def partner(x, axis):
    return lax.ppermute(x, axis, [(0, 1), (1, 0)])


def from_next(x, axis, distance):
    size = SIZES[AXES.index(axis)]
    return lax.ppermute(x, axis, [((i + distance) % size, i) for i in range(size)])


def local(student_in, weight, queries, keys, values, lengths, assignment):
    names = ("z", "yhi", "core", "ylo", "x")
    here = jnp.stack([lax.axis_index(a) for a in names]).astype(jnp.int32)
    wrows = weight.shape[0]

    lane = lax.broadcasted_iota(jnp.int32, (keys.shape[0], 2 * HD), 1)
    kv = jnp.where(
        lane < HD, jnp.pad(keys, ((0, 0), (0, HD))), jnp.pad(values, ((0, 0), (HD, 0)))
    )
    w_mine, w_other = halves(weight, here[3])
    kv_other = partner(kv, "yhi")
    w_parts = [
        w_mine,
        partner(w_other, "ylo"),
        partner(w_mine, "yhi"),
        lax.ppermute(w_other, ("ylo", "yhi"), [(i, 3 - i) for i in range(4)]),
    ]
    packed = pack(kv, kv_other, w_parts)

    student_in, _ = lax.optimization_barrier((student_in, packed))
    n_keep, n_send = normalise(here, student_in, wrows)
    up, down = from_next(packed, "z", 1), from_next(packed, "z", -1)
    up, down, n_keep, n_send = lax.optimization_barrier((up, down, n_keep, n_send))
    n_got, n_across = partner(n_send, "core"), partner(n_keep, "ylo")

    held = {0: packed, 1: up, -1: down}
    for d in range(2, 5):
        held[d] = from_next(held[d - 1], "z", 1)
        if d < 4:
            held[-d] = from_next(held[1 - d], "z", -1)
        if d == 2:
            held[2], held[-2], n_got = lax.optimization_barrier((held[2], held[-2], n_got))
        if d == 3:
            held[3], held[-3], n_across = lax.optimization_barrier((held[3], held[-3], n_across))
    n_all = jnp.concatenate([n_keep, n_got, n_across, partner(n_got, "ylo")], axis=0)
    parts = [held[d] for d in RING]
    w_rows = jnp.concatenate([part[2 * BLK :] for part in parts], axis=0)
    w_all = [w_rows] + [from_next(w_rows, "x", d) for d in range(1, 4)]

    parts, _ = lax.optimization_barrier((parts, w_rows))
    attention, a_mine, a_other = attend(here, queries, parts, lengths, assignment)

    own, send = project(here, n_all, a_mine, partner(a_other, "ylo"), w_all)
    near, *away = gradient(here, n_all, own, partner(send, "core"), wrows)
    near = near.astype(jnp.float32)
    for d in range(1, 4):
        near = near + from_next(away[d - 1], "x", d).astype(jnp.float32)
    near = near.astype(jnp.bfloat16).reshape(-1, wrows, HALF)
    near = jnp.pad(near, ((0, 0), (0, PADDED - wrows), (0, 0)))
    last = lax.all_to_all(near, ("ylo", *SEQ), split_axis=0, concat_axis=0, tiled=True)
    summed = last.reshape(2, 16, PADDED, HALF).astype(jnp.float32).sum(axis=1)
    weight_grad = jnp.concatenate([summed[0, :wrows], summed[1, :wrows]], axis=1)
    return (attention, weight_grad)


def solution(mesh):
    mesh = Mesh(mesh.devices.reshape(SIZES), AXES)
    token = P(AXES, None)
    row = P(("ylo", "x", "core"), None)
    return jax.shard_map(
        local,
        mesh=mesh,
        in_specs=(token, token, token, token, token, row, row),
        out_specs=(token, token),
        check_vma=False,
    )
```

```python
import math

import jax
import jax.numpy as jnp
from jax import lax
from jax.experimental import pallas as pl
from jax.experimental.pallas import tpu as pltpu
from jax.sharding import Mesh, PartitionSpec as P

HD = 128
HQ = 4
BLK = 128
COLS = HQ * HD
HALF = COLS // 2
TOKENS_ALL = 32768
PADDED = 16

EPSILON = 1e-06
NEGATIVE = -1e30
LOG2E = math.log2(math.e)

AXES = ("ylo", "x", "core", "z", "yhi")
SIZES = (2, 4, 2, 8, 2)
SEQ = ("z", "yhi")

RING = (0, 1, -1, 2, -2, 3, -3, 4)

SMEM = pl.BlockSpec(memory_space=pltpu.SMEM)
VMEM = pl.BlockSpec(memory_space=pltpu.VMEM)


def spread_tile(first, last, wide, wrows):
    target = lax.broadcasted_iota(jnp.int32, (1, wide), 1)
    inside = lax.rem(target, PADDED)
    target = jnp.where(inside < wrows, target // PADDED * wrows + inside, -1)
    source = lax.broadcasted_iota(jnp.int32, (last - first, 1), 0) + first
    return jnp.where(source == target, 1.0, 0.0).astype(jnp.bfloat16)


def normalise_kernel(where_ref, student_ref, keep_ref, send_ref, *, wrows):
    core = where_ref[2]
    rows, features = student_ref.shape
    group = 16 * PADDED
    taken = 16 * wrows
    chunk = features // 4
    as_float = student_ref[...].astype(jnp.float32)
    scale = lax.rsqrt(jnp.mean(as_float * as_float, axis=1, keepdims=True) + EPSILON)
    normed = (as_float * scale).astype(jnp.bfloat16)
    stacked = jnp.concatenate([normed[:, k * chunk : (k + 1) * chunk] for k in range(4)], axis=0)
    for q in range(chunk // taken):
        first = q * taken // 128 * 128
        last = min(chunk, -(-(q + 1) * taken // 128) * 128)
        tile = spread_tile(first - q * taken, last - q * taken, group, wrows)
        apart = jnp.dot(
            stacked[:, first:last], tile, preferred_element_type=jnp.float32
        ).astype(jnp.bfloat16)
        for k in range(4):
            g = k * (chunk // taken) + q
            at = (g // 2 % 4 * 2 + g // 8) * group
            piece = apart[k * rows : (k + 1) * rows]

            @pl.when(core == g % 2)
            def _():
                keep_ref[:, at : at + group] = piece

            @pl.when(core != g % 2)
            def _():
                send_ref[:, at : at + group] = piece


def normalise(here, student_in, wrows):
    rows, features = student_in.shape
    shape = jax.ShapeDtypeStruct((rows, features // wrows * PADDED // 2), jnp.bfloat16)

    def body(*refs):
        normalise_kernel(*refs, wrows=wrows)

    return pl.pallas_call(
        body,
        out_shape=(shape, shape),
        in_specs=[SMEM, VMEM],
        out_specs=(VMEM, VMEM),
        compiler_params=pltpu.CompilerParams(vmem_limit_bytes=16 << 20),
        name="normalise",
    )(here, student_in)


def pack_kernel(kv_ref, kv_other_ref, *refs):
    *w_refs, out_ref = refs
    rows = kv_ref.shape[0]
    wrows, width = w_refs[0].shape
    out_ref[:rows, :] = kv_ref[...]
    out_ref[rows : 2 * rows, :] = kv_other_ref[...]
    for i, w_ref in enumerate(w_refs):
        first = 2 * rows + i * PADDED
        out_ref[first : first + PADDED, :] = jnp.concatenate(
            [w_ref[...], jnp.zeros((PADDED - wrows, width), jnp.bfloat16)], axis=0
        )


def pack(kv, kv_other, w_parts):
    rows = 2 * kv.shape[0] + len(w_parts) * PADDED
    return pl.pallas_call(
        pack_kernel,
        out_shape=jax.ShapeDtypeStruct((rows, kv.shape[1]), jnp.bfloat16),
        in_specs=[VMEM] * (2 + len(w_parts)),
        out_specs=VMEM,
        compiler_params=pltpu.CompilerParams(vmem_limit_bytes=4 << 20),
        name="pack",
    )(kv, kv_other, *w_parts)


def attend_kernel(where_ref, assign_ref, length_ref, q_ref, *refs):
    *kv_refs, out_ref, mine_ref, other_ref, s_ref = refs
    z, yhi, ylo = where_ref[0], where_ref[1], where_ref[3]
    rows = q_ref.shape[0]
    own = assign_ref[0, 2 * z + yhi] * BLK
    first = length_ref[0, 0]
    second = first + length_ref[0, 1]
    third = second + length_ref[0, 2]
    q_pos = own + lax.broadcasted_iota(jnp.int32, (rows, 1), 0)
    q_start = jnp.where(
        q_pos >= third,
        third,
        jnp.where(q_pos >= second, second, jnp.where(q_pos >= first, first, 0)),
    )
    q_all = jnp.concatenate([q_ref[:, h * HD : (h + 1) * HD] for h in range(HQ)], axis=0)
    lane = lax.broadcasted_iota(jnp.int32, (1, BLK), 1)
    chunk = 2 * BLK
    top = None
    for c, (distance, kv_ref) in enumerate(zip(RING, kv_refs)):
        pair = lax.rem(z + distance + 8, 8) * 2
        k_pos = [assign_ref[0, pair + yhi] * BLK + lane, assign_ref[0, pair + 1 - yhi] * BLK + lane]
        k_pos = jnp.concatenate(k_pos, axis=1)
        bias = jnp.where((k_pos >= q_start) & (k_pos <= q_pos), 0.0, NEGATIVE)
        scores = lax.dot_general(
            q_all,
            kv_ref[:chunk, :HD],
            (((1,), (1,)), ((), ())),
            preferred_element_type=jnp.float32,
        )
        scores = scores.reshape(HQ, rows, chunk) * (HD ** (-0.5) * LOG2E) + bias[None]
        scores = scores.reshape(HQ * rows, chunk)
        s_ref[:, c * chunk : (c + 1) * chunk] = scores
        best = jnp.max(scores, axis=1, keepdims=True)
        top = best if top is None else jnp.maximum(top, best)
    total = jnp.zeros((HQ * rows, 1), jnp.float32)
    mixture = jnp.zeros((HQ * rows, HD), jnp.float32)
    for c, kv_ref in enumerate(kv_refs):
        terms = jnp.exp2(s_ref[:, c * chunk : (c + 1) * chunk] - top)
        total = total + jnp.sum(terms, axis=1, keepdims=True)
        mixture = mixture + jnp.dot(
            terms.astype(jnp.bfloat16), kv_ref[:chunk, HD:], preferred_element_type=jnp.float32
        )
    result = (mixture / total).astype(jnp.bfloat16)
    for h in range(HQ):
        head = result[h * rows : (h + 1) * rows]
        out_ref[:, h * HD : (h + 1) * HD] = head
        at = h % (HQ // 2) * HD

        @pl.when(ylo == h // (HQ // 2))
        def _():
            mine_ref[:, at : at + HD] = head

        @pl.when(ylo != h // (HQ // 2))
        def _():
            other_ref[:, at : at + HD] = head


def attend(here, queries, parts, lengths, assignment):
    rows = queries.shape[0]
    half = jax.ShapeDtypeStruct((rows, HALF), jnp.bfloat16)
    return pl.pallas_call(
        attend_kernel,
        out_shape=(jax.ShapeDtypeStruct((rows, COLS), jnp.bfloat16), half, half),
        in_specs=[SMEM, SMEM, SMEM, VMEM] + [VMEM] * len(parts),
        out_specs=(VMEM, VMEM, VMEM),
        scratch_shapes=[pltpu.VMEM((HQ * rows, 16 * BLK), jnp.float32)],
        compiler_params=pltpu.CompilerParams(vmem_limit_bytes=20 << 20),
        name="attend",
    )(here, assignment, lengths, queries, *parts)


def project_kernel(where_ref, n_ref, mine_ref, got_ref, *refs):
    *w_refs, own_ref, send_ref, w_all = refs
    z, yhi, ylo, x = where_ref[0], where_ref[1], where_ref[3], where_ref[4]
    group = 16 * PADDED
    for d in range(4):
        at_x = lax.rem(x + d, 4) * 2
        for k, distance in enumerate(RING):
            pair = lax.rem(z + distance + 8, 8) * 2
            for t in range(2):
                slot = pair + (yhi if t == 0 else 1 - yhi)
                for i in range(2):
                    side = ylo if i == 0 else 1 - ylo
                    at = (at_x + side) * group + slot * PADDED
                    first = (k * 4 + t * 2 + i) * PADDED
                    w_all[pl.ds(pl.multiple_of(at, PADDED), PADDED), :] = w_refs[d][
                        first : first + PADDED, :
                    ]
    rows = n_ref.shape[0] // 4
    for b in range(4):
        part = jnp.dot(
            n_ref[b * rows : (b + 1) * rows, :], w_all[...], preferred_element_type=jnp.float32
        )
        if b % 2 == 0:
            part = part - (mine_ref, got_ref)[b // 2][...].astype(jnp.float32)
        own_ref[b * rows : (b + 1) * rows, :] = part
        t = b ^ 1
        send_ref[t * rows : (t + 1) * rows, :] = part.astype(jnp.bfloat16)


def project(here, n_all, a_mine, a_got, w_parts):
    shape = (n_all.shape[0], HALF)
    return pl.pallas_call(
        project_kernel,
        out_shape=(
            jax.ShapeDtypeStruct(shape, jnp.float32),
            jax.ShapeDtypeStruct(shape, jnp.bfloat16),
        ),
        in_specs=[SMEM] + [VMEM] * (3 + len(w_parts)),
        out_specs=(VMEM, VMEM),
        scratch_shapes=[pltpu.VMEM((n_all.shape[1], HALF), jnp.bfloat16)],
        compiler_params=pltpu.CompilerParams(vmem_limit_bytes=12 << 20),
        name="project",
    )(here, n_all, a_mine, a_got, *w_parts)


def halves(x, which):
    half = x.shape[1] // 2
    low, high = x[:, :half], x[:, half:]
    return jnp.where(which == 0, low, high), jnp.where(which == 0, high, low)


def gradient_kernel(where_ref, n_ref, own_ref, back_ref, *out_refs):
    x = where_ref[4]
    columns = n_ref.shape[1] // 4
    taken = out_refs[0].shape[0]
    wrows = taken * PADDED // columns
    diff = own_ref[...] + back_ref[...].astype(jnp.float32)
    scaled = (diff * TOKENS_ALL ** (-0.5)).astype(jnp.bfloat16)
    step = 128 // PADDED * wrows
    target = lax.broadcasted_iota(jnp.int32, (1, 128), 1)
    inside = lax.rem(target, PADDED)
    target = jnp.where(inside < wrows, target // PADDED * wrows + inside, -1)
    row = lax.broadcasted_iota(jnp.int32, (step, 1), 0)
    cut = jnp.where(row == target, 1.0, 0.0).astype(jnp.bfloat16)
    for d, out_ref in enumerate(out_refs):
        at = pl.multiple_of(lax.rem(x + 4 - d, 4) * columns, columns)
        part = lax.dot_general(
            n_ref[:, pl.ds(at, columns)],
            scaled,
            (((0,), (0,)), ((), ())),
            preferred_element_type=jnp.float32,
        ).astype(jnp.bfloat16)
        for j in range(columns // 128):
            out_ref[j * step : (j + 1) * step, :] = jnp.dot(
                cut, part[j * 128 : (j + 1) * 128], preferred_element_type=jnp.float32
            ).astype(jnp.bfloat16)


def gradient(here, n_all, own, back, wrows):
    shape = jax.ShapeDtypeStruct((n_all.shape[1] // 4 // PADDED * wrows, HALF), jnp.bfloat16)
    return pl.pallas_call(
        gradient_kernel,
        out_shape=(shape,) * 4,
        in_specs=[SMEM, VMEM, VMEM, VMEM],
        out_specs=(VMEM,) * 4,
        compiler_params=pltpu.CompilerParams(vmem_limit_bytes=16 << 20),
        name="gradient",
    )(here, n_all, own, back)


def partner(x, axis):
    return lax.ppermute(x, axis, [(0, 1), (1, 0)])


def from_next(x, axis, distance):
    size = SIZES[AXES.index(axis)]
    return lax.ppermute(x, axis, [((i + distance) % size, i) for i in range(size)])


def local(student_in, weight, queries, keys, values, lengths, assignment):
    names = ("z", "yhi", "core", "ylo", "x")
    here = jnp.stack([lax.axis_index(a) for a in names]).astype(jnp.int32)
    wrows = weight.shape[0]

    lane = lax.broadcasted_iota(jnp.int32, (keys.shape[0], 2 * HD), 1)
    kv = jnp.where(
        lane < HD, jnp.pad(keys, ((0, 0), (0, HD))), jnp.pad(values, ((0, 0), (HD, 0)))
    )
    w_mine, w_other = halves(weight, here[3])
    kv_other = partner(kv, "yhi")
    w_parts = [
        w_mine,
        partner(w_other, "ylo"),
        partner(w_mine, "yhi"),
        lax.ppermute(w_other, ("ylo", "yhi"), [(i, 3 - i) for i in range(4)]),
    ]
    packed = pack(kv, kv_other, w_parts)

    student_in, _ = lax.optimization_barrier((student_in, packed))
    n_keep, n_send = normalise(here, student_in, wrows)
    up, down = from_next(packed, "z", 1), from_next(packed, "z", -1)
    up, down, n_keep, n_send = lax.optimization_barrier((up, down, n_keep, n_send))
    n_got, n_across = partner(n_send, "core"), partner(n_keep, "ylo")

    held = {0: packed, 1: up, -1: down}
    for d in range(2, 5):
        held[d] = from_next(held[d - 1], "z", 1)
        if d < 4:
            held[-d] = from_next(held[1 - d], "z", -1)
        if d == 2:
            held[2], held[-2], n_got = lax.optimization_barrier((held[2], held[-2], n_got))
    n_all = jnp.concatenate([n_keep, n_got, n_across, partner(n_got, "ylo")], axis=0)
    parts = [held[d] for d in RING]
    w_rows = jnp.concatenate([part[2 * BLK :] for part in parts], axis=0)
    w_all = [w_rows] + [from_next(w_rows, "x", d) for d in range(1, 4)]

    parts, _ = lax.optimization_barrier((parts, (w_rows, n_across)))
    attention, a_mine, a_other = attend(here, queries, parts, lengths, assignment)

    own, send = project(here, n_all, a_mine, partner(a_other, "ylo"), w_all)
    near, *away = gradient(here, n_all, own, partner(send, "core"), wrows)
    near = near.astype(jnp.float32)
    for d in range(1, 4):
        near = near + from_next(away[d - 1], "x", d).astype(jnp.float32)
    near = near.astype(jnp.bfloat16).reshape(-1, wrows, HALF)
    near = jnp.pad(near, ((0, 0), (0, PADDED - wrows), (0, 0)))
    last = lax.all_to_all(near, ("ylo", *SEQ), split_axis=0, concat_axis=0, tiled=True)
    summed = last.reshape(2, 16, PADDED, HALF).astype(jnp.float32).sum(axis=1)
    weight_grad = jnp.concatenate([summed[0, :wrows], summed[1, :wrows]], axis=1)
    return (attention, weight_grad)


def solution(mesh):
    mesh = Mesh(mesh.devices.reshape(SIZES), AXES)
    token = P(AXES, None)
    row = P(("ylo", "x", "core"), None)
    return jax.shard_map(
        local,
        mesh=mesh,
        in_specs=(token, token, token, token, token, row, row),
        out_specs=(token, token),
        check_vma=False,
    )
```

```python
import math

import jax
import jax.numpy as jnp
from jax import lax
from jax.experimental import pallas as pl
from jax.experimental.pallas import tpu as pltpu
from jax.sharding import Mesh, PartitionSpec as P

HD = 128
HQ = 4
BLK = 128
COLS = HQ * HD
HALF = COLS // 2
TOKENS_ALL = 32768
PADDED = 16

EPSILON = 1e-06
NEGATIVE = -1e30
LOG2E = math.log2(math.e)

AXES = ("ylo", "x", "core", "z", "yhi")
SIZES = (2, 4, 2, 8, 2)
SEQ = ("z", "yhi")

RING = (0, 1, -1, 2, -2, 3, -3, 4)

SMEM = pl.BlockSpec(memory_space=pltpu.SMEM)
VMEM = pl.BlockSpec(memory_space=pltpu.VMEM)


def spread_tile(first, last, wide, wrows):
    target = lax.broadcasted_iota(jnp.int32, (1, wide), 1)
    inside = lax.rem(target, PADDED)
    target = jnp.where(inside < wrows, target // PADDED * wrows + inside, -1)
    source = lax.broadcasted_iota(jnp.int32, (last - first, 1), 0) + first
    return jnp.where(source == target, 1.0, 0.0).astype(jnp.bfloat16)


def normalise_kernel(where_ref, student_ref, keep_ref, send_ref, *, wrows):
    core = where_ref[2]
    rows, features = student_ref.shape
    group = 16 * PADDED
    taken = 16 * wrows
    chunk = features // 4
    as_float = student_ref[...].astype(jnp.float32)
    scale = lax.rsqrt(jnp.mean(as_float * as_float, axis=1, keepdims=True) + EPSILON)
    normed = (as_float * scale).astype(jnp.bfloat16)
    stacked = jnp.concatenate([normed[:, k * chunk : (k + 1) * chunk] for k in range(4)], axis=0)
    for q in range(chunk // taken):
        first = q * taken // 128 * 128
        last = min(chunk, -(-(q + 1) * taken // 128) * 128)
        tile = spread_tile(first - q * taken, last - q * taken, group, wrows)
        apart = jnp.dot(
            stacked[:, first:last], tile, preferred_element_type=jnp.float32
        ).astype(jnp.bfloat16)
        for k in range(4):
            g = k * (chunk // taken) + q
            at = (g // 2 % 4 * 2 + g // 8) * group
            piece = apart[k * rows : (k + 1) * rows]

            @pl.when(core == g % 2)
            def _():
                keep_ref[:, at : at + group] = piece

            @pl.when(core != g % 2)
            def _():
                send_ref[:, at : at + group] = piece


def normalise(here, student_in, wrows):
    rows, features = student_in.shape
    shape = jax.ShapeDtypeStruct((rows, features // wrows * PADDED // 2), jnp.bfloat16)

    def body(*refs):
        normalise_kernel(*refs, wrows=wrows)

    return pl.pallas_call(
        body,
        out_shape=(shape, shape),
        in_specs=[SMEM, VMEM],
        out_specs=(VMEM, VMEM),
        compiler_params=pltpu.CompilerParams(vmem_limit_bytes=16 << 20),
        name="normalise",
    )(here, student_in)


def pack_kernel(kv_ref, kv_other_ref, *refs):
    *w_refs, out_ref = refs
    rows = kv_ref.shape[0]
    wrows, width = w_refs[0].shape
    out_ref[:rows, :] = kv_ref[...]
    out_ref[rows : 2 * rows, :] = kv_other_ref[...]
    for i, w_ref in enumerate(w_refs):
        first = 2 * rows + i * PADDED
        out_ref[first : first + PADDED, :] = jnp.concatenate(
            [w_ref[...], jnp.zeros((PADDED - wrows, width), jnp.bfloat16)], axis=0
        )


def pack(kv, kv_other, w_parts):
    rows = 2 * kv.shape[0] + len(w_parts) * PADDED
    return pl.pallas_call(
        pack_kernel,
        out_shape=jax.ShapeDtypeStruct((rows, kv.shape[1]), jnp.bfloat16),
        in_specs=[VMEM] * (2 + len(w_parts)),
        out_specs=VMEM,
        compiler_params=pltpu.CompilerParams(vmem_limit_bytes=4 << 20),
        name="pack",
    )(kv, kv_other, *w_parts)


def attend_kernel(where_ref, assign_ref, length_ref, q_ref, *refs):
    *kv_refs, out_ref, mine_ref, other_ref, s_ref = refs
    z, yhi, ylo = where_ref[0], where_ref[1], where_ref[3]
    rows = q_ref.shape[0]
    own = assign_ref[0, 2 * z + yhi] * BLK
    first = length_ref[0, 0]
    second = first + length_ref[0, 1]
    third = second + length_ref[0, 2]
    q_pos = own + lax.broadcasted_iota(jnp.int32, (rows, 1), 0)
    q_start = jnp.where(
        q_pos >= third,
        third,
        jnp.where(q_pos >= second, second, jnp.where(q_pos >= first, first, 0)),
    )
    q_all = jnp.concatenate([q_ref[:, h * HD : (h + 1) * HD] for h in range(HQ)], axis=0)
    lane = lax.broadcasted_iota(jnp.int32, (1, BLK), 1)
    chunk = 2 * BLK
    top = None
    for c, (distance, kv_ref) in enumerate(zip(RING, kv_refs)):
        pair = lax.rem(z + distance + 8, 8) * 2
        k_pos = [assign_ref[0, pair + yhi] * BLK + lane, assign_ref[0, pair + 1 - yhi] * BLK + lane]
        k_pos = jnp.concatenate(k_pos, axis=1)
        bias = jnp.where((k_pos >= q_start) & (k_pos <= q_pos), 0.0, NEGATIVE)
        scores = lax.dot_general(
            q_all,
            kv_ref[:chunk, :HD],
            (((1,), (1,)), ((), ())),
            preferred_element_type=jnp.float32,
        )
        scores = scores.reshape(HQ, rows, chunk) * (HD ** (-0.5) * LOG2E) + bias[None]
        scores = scores.reshape(HQ * rows, chunk)
        s_ref[:, c * chunk : (c + 1) * chunk] = scores
        best = jnp.max(scores, axis=1, keepdims=True)
        top = best if top is None else jnp.maximum(top, best)
    total = jnp.zeros((HQ * rows, 1), jnp.float32)
    mixture = jnp.zeros((HQ * rows, HD), jnp.float32)
    for c, kv_ref in enumerate(kv_refs):
        terms = jnp.exp2(s_ref[:, c * chunk : (c + 1) * chunk] - top)
        total = total + jnp.sum(terms, axis=1, keepdims=True)
        mixture = mixture + jnp.dot(
            terms.astype(jnp.bfloat16), kv_ref[:chunk, HD:], preferred_element_type=jnp.float32
        )
    result = (mixture / total).astype(jnp.bfloat16)
    for h in range(HQ):
        head = result[h * rows : (h + 1) * rows]
        out_ref[:, h * HD : (h + 1) * HD] = head
        at = h % (HQ // 2) * HD

        @pl.when(ylo == h // (HQ // 2))
        def _():
            mine_ref[:, at : at + HD] = head

        @pl.when(ylo != h // (HQ // 2))
        def _():
            other_ref[:, at : at + HD] = head


def attend(here, queries, parts, lengths, assignment):
    rows = queries.shape[0]
    half = jax.ShapeDtypeStruct((rows, HALF), jnp.bfloat16)
    return pl.pallas_call(
        attend_kernel,
        out_shape=(jax.ShapeDtypeStruct((rows, COLS), jnp.bfloat16), half, half),
        in_specs=[SMEM, SMEM, SMEM, VMEM] + [VMEM] * len(parts),
        out_specs=(VMEM, VMEM, VMEM),
        scratch_shapes=[pltpu.VMEM((HQ * rows, 16 * BLK), jnp.float32)],
        compiler_params=pltpu.CompilerParams(vmem_limit_bytes=20 << 20),
        name="attend",
    )(here, assignment, lengths, queries, *parts)


def project_kernel(where_ref, n_ref, mine_ref, got_ref, *refs):
    *w_refs, own_ref, send_ref, w_all = refs
    z, yhi, ylo, x = where_ref[0], where_ref[1], where_ref[3], where_ref[4]
    group = 16 * PADDED
    for d in range(4):
        at_x = lax.rem(x + d, 4) * 2
        for k, distance in enumerate(RING):
            pair = lax.rem(z + distance + 8, 8) * 2
            for t in range(2):
                slot = pair + (yhi if t == 0 else 1 - yhi)
                for i in range(2):
                    side = ylo if i == 0 else 1 - ylo
                    at = (at_x + side) * group + slot * PADDED
                    first = (k * 4 + t * 2 + i) * PADDED
                    w_all[pl.ds(pl.multiple_of(at, PADDED), PADDED), :] = w_refs[d][
                        first : first + PADDED, :
                    ]
    rows = n_ref.shape[0] // 4
    for b in range(4):
        part = jnp.dot(
            n_ref[b * rows : (b + 1) * rows, :], w_all[...], preferred_element_type=jnp.float32
        )
        if b % 2 == 0:
            part = part - (mine_ref, got_ref)[b // 2][...].astype(jnp.float32)
        own_ref[b * rows : (b + 1) * rows, :] = part
        t = b ^ 1
        send_ref[t * rows : (t + 1) * rows, :] = part.astype(jnp.bfloat16)


def project(here, n_all, a_mine, a_got, w_parts):
    shape = (n_all.shape[0], HALF)
    return pl.pallas_call(
        project_kernel,
        out_shape=(
            jax.ShapeDtypeStruct(shape, jnp.float32),
            jax.ShapeDtypeStruct(shape, jnp.bfloat16),
        ),
        in_specs=[SMEM] + [VMEM] * (3 + len(w_parts)),
        out_specs=(VMEM, VMEM),
        scratch_shapes=[pltpu.VMEM((n_all.shape[1], HALF), jnp.bfloat16)],
        compiler_params=pltpu.CompilerParams(vmem_limit_bytes=12 << 20),
        name="project",
    )(here, n_all, a_mine, a_got, *w_parts)


def halves(x, which):
    half = x.shape[1] // 2
    low, high = x[:, :half], x[:, half:]
    return jnp.where(which == 0, low, high), jnp.where(which == 0, high, low)


def gradient_kernel(where_ref, n_ref, own_ref, back_ref, *out_refs, steps):
    x = where_ref[4]
    columns = n_ref.shape[1] // 4
    taken = out_refs[0].shape[0]
    wrows = taken * PADDED // columns
    diff = own_ref[...] + back_ref[...].astype(jnp.float32)
    scaled = (diff * TOKENS_ALL ** (-0.5)).astype(jnp.bfloat16)
    step = 128 // PADDED * wrows
    target = lax.broadcasted_iota(jnp.int32, (1, 128), 1)
    inside = lax.rem(target, PADDED)
    target = jnp.where(inside < wrows, target // PADDED * wrows + inside, -1)
    row = lax.broadcasted_iota(jnp.int32, (step, 1), 0)
    cut = jnp.where(row == target, 1.0, 0.0).astype(jnp.bfloat16)
    for d, out_ref in zip(steps, out_refs):
        at = pl.multiple_of(lax.rem(x + 4 - d, 4) * columns, columns)
        part = lax.dot_general(
            n_ref[:, pl.ds(at, columns)],
            scaled,
            (((0,), (0,)), ((), ())),
            preferred_element_type=jnp.float32,
        ).astype(jnp.bfloat16)
        for j in range(columns // 128):
            out_ref[j * step : (j + 1) * step, :] = jnp.dot(
                cut, part[j * 128 : (j + 1) * 128], preferred_element_type=jnp.float32
            ).astype(jnp.bfloat16)


def gradient(here, n_all, own, back, wrows, steps):
    shape = jax.ShapeDtypeStruct((n_all.shape[1] // 4 // PADDED * wrows, HALF), jnp.bfloat16)

    def body(*refs):
        gradient_kernel(*refs, steps=steps)

    return pl.pallas_call(
        body,
        out_shape=(shape,) * len(steps),
        in_specs=[SMEM, VMEM, VMEM, VMEM],
        out_specs=(VMEM,) * len(steps),
        compiler_params=pltpu.CompilerParams(vmem_limit_bytes=16 << 20),
        name="gradient",
    )(here, n_all, own, back)


def partner(x, axis):
    return lax.ppermute(x, axis, [(0, 1), (1, 0)])


def from_next(x, axis, distance):
    size = SIZES[AXES.index(axis)]
    return lax.ppermute(x, axis, [((i + distance) % size, i) for i in range(size)])


def local(student_in, weight, queries, keys, values, lengths, assignment):
    names = ("z", "yhi", "core", "ylo", "x")
    here = jnp.stack([lax.axis_index(a) for a in names]).astype(jnp.int32)
    wrows = weight.shape[0]

    lane = lax.broadcasted_iota(jnp.int32, (keys.shape[0], 2 * HD), 1)
    kv = jnp.where(
        lane < HD, jnp.pad(keys, ((0, 0), (0, HD))), jnp.pad(values, ((0, 0), (HD, 0)))
    )
    w_mine, w_other = halves(weight, here[3])
    kv_other = partner(kv, "yhi")
    w_parts = [
        w_mine,
        partner(w_other, "ylo"),
        partner(w_mine, "yhi"),
        lax.ppermute(w_other, ("ylo", "yhi"), [(i, 3 - i) for i in range(4)]),
    ]
    packed = pack(kv, kv_other, w_parts)

    student_in, _ = lax.optimization_barrier((student_in, packed))
    n_keep, n_send = normalise(here, student_in, wrows)
    up, down = from_next(packed, "z", 1), from_next(packed, "z", -1)
    up, down, n_keep, n_send = lax.optimization_barrier((up, down, n_keep, n_send))
    n_got, n_across = partner(n_send, "core"), partner(n_keep, "ylo")

    held = {0: packed, 1: up, -1: down}
    for d in range(2, 5):
        held[d] = from_next(held[d - 1], "z", 1)
        if d < 4:
            held[-d] = from_next(held[1 - d], "z", -1)
        if d == 2:
            held[2], held[-2], n_got = lax.optimization_barrier((held[2], held[-2], n_got))
    n_all = jnp.concatenate([n_keep, n_got, n_across, partner(n_got, "ylo")], axis=0)
    parts = [held[d] for d in RING]
    w_rows = jnp.concatenate([part[2 * BLK :] for part in parts], axis=0)
    w_sent = {d: from_next(w_rows, "x", d) for d in (2, 1, 3)}
    w_all = [w_rows] + [w_sent[d] for d in range(1, 4)]

    parts, _ = lax.optimization_barrier((parts, (w_rows, n_across)))
    attention, a_mine, a_other = attend(here, queries, parts, lengths, assignment)

    own, send = project(here, n_all, a_mine, partner(a_other, "ylo"), w_all)
    back = partner(send, "core")
    far, left = gradient(here, n_all, own, back, wrows, (2, 3))
    arrived = [from_next(left, "x", 3), from_next(far, "x", 2)]
    back, _ = lax.optimization_barrier((back, far))
    near, right = gradient(here, n_all, own, back, wrows, (0, 1))
    arrived.append(from_next(right, "x", 1))
    near = near.astype(jnp.float32)
    for block in arrived:
        near = near + block.astype(jnp.float32)
    near = near.astype(jnp.bfloat16).reshape(-1, wrows, HALF)
    near = jnp.pad(near, ((0, 0), (0, PADDED - wrows), (0, 0)))
    last = lax.all_to_all(near, ("ylo", *SEQ), split_axis=0, concat_axis=0, tiled=True)
    summed = last.reshape(2, 16, PADDED, HALF).astype(jnp.float32).sum(axis=1)
    weight_grad = jnp.concatenate([summed[0, :wrows], summed[1, :wrows]], axis=1)
    return (attention, weight_grad)


def solution(mesh):
    mesh = Mesh(mesh.devices.reshape(SIZES), AXES)
    token = P(AXES, None)
    row = P(("ylo", "x", "core"), None)
    return jax.shard_map(
        local,
        mesh=mesh,
        in_specs=(token, token, token, token, token, row, row),
        out_specs=(token, token),
        check_vma=False,
    )
```

```python
import math

import jax
import jax.numpy as jnp
from jax import lax
from jax.experimental import pallas as pl
from jax.experimental.pallas import tpu as pltpu
from jax.sharding import Mesh, PartitionSpec as P

HD = 128
HQ = 4
BLK = 128
COLS = HQ * HD
HALF = COLS // 2
TOKENS_ALL = 32768
PADDED = 16

EPSILON = 1e-06
NEGATIVE = -1e30
LOG2E = math.log2(math.e)

AXES = ("ylo", "x", "core", "z", "yhi")
SIZES = (2, 4, 2, 8, 2)
SEQ = ("z", "yhi")

RING = (0, 1, -1, 2, -2, 3, -3, 4)

SMEM = pl.BlockSpec(memory_space=pltpu.SMEM)
VMEM = pl.BlockSpec(memory_space=pltpu.VMEM)


def spread_tile(first, last, wide, wrows):
    target = lax.broadcasted_iota(jnp.int32, (1, wide), 1)
    inside = lax.rem(target, PADDED)
    target = jnp.where(inside < wrows, target // PADDED * wrows + inside, -1)
    source = lax.broadcasted_iota(jnp.int32, (last - first, 1), 0) + first
    return jnp.where(source == target, 1.0, 0.0).astype(jnp.bfloat16)


def normalise_kernel(where_ref, student_ref, keep_ref, send_ref, *, wrows):
    core = where_ref[2]
    rows, features = student_ref.shape
    group = 16 * PADDED
    taken = 16 * wrows
    chunk = features // 4
    as_float = student_ref[...].astype(jnp.float32)
    scale = lax.rsqrt(jnp.mean(as_float * as_float, axis=1, keepdims=True) + EPSILON)
    normed = (as_float * scale).astype(jnp.bfloat16)
    stacked = jnp.concatenate([normed[:, k * chunk : (k + 1) * chunk] for k in range(4)], axis=0)
    for q in range(chunk // taken):
        first = q * taken // 128 * 128
        last = min(chunk, -(-(q + 1) * taken // 128) * 128)
        tile = spread_tile(first - q * taken, last - q * taken, group, wrows)
        apart = jnp.dot(
            stacked[:, first:last], tile, preferred_element_type=jnp.float32
        ).astype(jnp.bfloat16)
        for k in range(4):
            g = k * (chunk // taken) + q
            at = (g // 2 % 4 * 2 + g // 8) * group
            piece = apart[k * rows : (k + 1) * rows]

            @pl.when(core == g % 2)
            def _():
                keep_ref[:, at : at + group] = piece

            @pl.when(core != g % 2)
            def _():
                send_ref[:, at : at + group] = piece


def normalise(here, student_in, wrows):
    rows, features = student_in.shape
    shape = jax.ShapeDtypeStruct((rows, features // wrows * PADDED // 2), jnp.bfloat16)

    def body(*refs):
        normalise_kernel(*refs, wrows=wrows)

    return pl.pallas_call(
        body,
        out_shape=(shape, shape),
        in_specs=[SMEM, VMEM],
        out_specs=(VMEM, VMEM),
        compiler_params=pltpu.CompilerParams(vmem_limit_bytes=16 << 20),
        name="normalise",
    )(here, student_in)


def pack_kernel(kv_ref, kv_other_ref, *refs):
    *w_refs, out_ref = refs
    rows = kv_ref.shape[0]
    wrows, width = w_refs[0].shape
    out_ref[:rows, :] = kv_ref[...]
    out_ref[rows : 2 * rows, :] = kv_other_ref[...]
    for i, w_ref in enumerate(w_refs):
        first = 2 * rows + i * PADDED
        out_ref[first : first + PADDED, :] = jnp.concatenate(
            [w_ref[...], jnp.zeros((PADDED - wrows, width), jnp.bfloat16)], axis=0
        )


def pack(kv, kv_other, w_parts):
    rows = 2 * kv.shape[0] + len(w_parts) * PADDED
    return pl.pallas_call(
        pack_kernel,
        out_shape=jax.ShapeDtypeStruct((rows, kv.shape[1]), jnp.bfloat16),
        in_specs=[VMEM] * (2 + len(w_parts)),
        out_specs=VMEM,
        compiler_params=pltpu.CompilerParams(vmem_limit_bytes=4 << 20),
        name="pack",
    )(kv, kv_other, *w_parts)


def attend_kernel(where_ref, assign_ref, length_ref, q_ref, *refs):
    *kv_refs, out_ref, mine_ref, other_ref, s_ref = refs
    z, yhi, ylo = where_ref[0], where_ref[1], where_ref[3]
    rows = q_ref.shape[0]
    own = assign_ref[0, 2 * z + yhi] * BLK
    first = length_ref[0, 0]
    second = first + length_ref[0, 1]
    third = second + length_ref[0, 2]
    q_pos = own + lax.broadcasted_iota(jnp.int32, (rows, 1), 0)
    q_start = jnp.where(
        q_pos >= third,
        third,
        jnp.where(q_pos >= second, second, jnp.where(q_pos >= first, first, 0)),
    )
    q_all = jnp.concatenate([q_ref[:, h * HD : (h + 1) * HD] for h in range(HQ)], axis=0)
    lane = lax.broadcasted_iota(jnp.int32, (1, BLK), 1)
    chunk = 2 * BLK
    top = None
    for c, (distance, kv_ref) in enumerate(zip(RING, kv_refs)):
        pair = lax.rem(z + distance + 8, 8) * 2
        k_pos = [assign_ref[0, pair + yhi] * BLK + lane, assign_ref[0, pair + 1 - yhi] * BLK + lane]
        k_pos = jnp.concatenate(k_pos, axis=1)
        bias = jnp.where((k_pos >= q_start) & (k_pos <= q_pos), 0.0, NEGATIVE)
        scores = lax.dot_general(
            q_all,
            kv_ref[:chunk, :HD],
            (((1,), (1,)), ((), ())),
            preferred_element_type=jnp.float32,
        )
        scores = scores.reshape(HQ, rows, chunk) * (HD ** (-0.5) * LOG2E) + bias[None]
        scores = scores.reshape(HQ * rows, chunk)
        s_ref[:, c * chunk : (c + 1) * chunk] = scores
        best = jnp.max(scores, axis=1, keepdims=True)
        top = best if top is None else jnp.maximum(top, best)
    total = jnp.zeros((HQ * rows, 1), jnp.float32)
    mixture = jnp.zeros((HQ * rows, HD), jnp.float32)
    for c, kv_ref in enumerate(kv_refs):
        terms = jnp.exp2(s_ref[:, c * chunk : (c + 1) * chunk] - top)
        total = total + jnp.sum(terms, axis=1, keepdims=True)
        mixture = mixture + jnp.dot(
            terms.astype(jnp.bfloat16), kv_ref[:chunk, HD:], preferred_element_type=jnp.float32
        )
    result = (mixture / total).astype(jnp.bfloat16)
    for h in range(HQ):
        head = result[h * rows : (h + 1) * rows]
        out_ref[:, h * HD : (h + 1) * HD] = head
        at = h % (HQ // 2) * HD

        @pl.when(ylo == h // (HQ // 2))
        def _():
            mine_ref[:, at : at + HD] = head

        @pl.when(ylo != h // (HQ // 2))
        def _():
            other_ref[:, at : at + HD] = head


def attend(here, queries, parts, lengths, assignment):
    rows = queries.shape[0]
    half = jax.ShapeDtypeStruct((rows, HALF), jnp.bfloat16)
    return pl.pallas_call(
        attend_kernel,
        out_shape=(jax.ShapeDtypeStruct((rows, COLS), jnp.bfloat16), half, half),
        in_specs=[SMEM, SMEM, SMEM, VMEM] + [VMEM] * len(parts),
        out_specs=(VMEM, VMEM, VMEM),
        scratch_shapes=[pltpu.VMEM((HQ * rows, 16 * BLK), jnp.float32)],
        compiler_params=pltpu.CompilerParams(vmem_limit_bytes=20 << 20),
        name="attend",
    )(here, assignment, lengths, queries, *parts)


def project_kernel(where_ref, n_ref, mine_ref, got_ref, *refs):
    *w_refs, own_ref, send_ref, w_all = refs
    z, yhi, ylo, x = where_ref[0], where_ref[1], where_ref[3], where_ref[4]
    group = 16 * PADDED
    for d in range(4):
        at_x = lax.rem(x + d, 4) * 2
        for k, distance in enumerate(RING):
            pair = lax.rem(z + distance + 8, 8) * 2
            for t in range(2):
                slot = pair + (yhi if t == 0 else 1 - yhi)
                for i in range(2):
                    side = ylo if i == 0 else 1 - ylo
                    at = (at_x + side) * group + slot * PADDED
                    first = (k * 4 + t * 2 + i) * PADDED
                    w_all[pl.ds(pl.multiple_of(at, PADDED), PADDED), :] = w_refs[d][
                        first : first + PADDED, :
                    ]
    rows = n_ref.shape[0] // 4
    for b in range(4):
        part = jnp.dot(
            n_ref[b * rows : (b + 1) * rows, :], w_all[...], preferred_element_type=jnp.float32
        )
        if b % 2 == 0:
            part = part - (mine_ref, got_ref)[b // 2][...].astype(jnp.float32)
        own_ref[b * rows : (b + 1) * rows, :] = part
        t = b ^ 1
        send_ref[t * rows : (t + 1) * rows, :] = part.astype(jnp.bfloat16)


def project(here, n_all, a_mine, a_got, w_parts):
    shape = (n_all.shape[0], HALF)
    return pl.pallas_call(
        project_kernel,
        out_shape=(
            jax.ShapeDtypeStruct(shape, jnp.float32),
            jax.ShapeDtypeStruct(shape, jnp.bfloat16),
        ),
        in_specs=[SMEM] + [VMEM] * (3 + len(w_parts)),
        out_specs=(VMEM, VMEM),
        scratch_shapes=[pltpu.VMEM((n_all.shape[1], HALF), jnp.bfloat16)],
        compiler_params=pltpu.CompilerParams(vmem_limit_bytes=12 << 20),
        name="project",
    )(here, n_all, a_mine, a_got, *w_parts)


def halves(x, which):
    half = x.shape[1] // 2
    low, high = x[:, :half], x[:, half:]
    return jnp.where(which == 0, low, high), jnp.where(which == 0, high, low)


def gradient_kernel(where_ref, n_ref, own_ref, back_ref, *out_refs, steps):
    x = where_ref[4]
    columns = n_ref.shape[1] // 4
    taken = out_refs[0].shape[0]
    wrows = taken * PADDED // columns
    diff = own_ref[...] + back_ref[...].astype(jnp.float32)
    scaled = (diff * TOKENS_ALL ** (-0.5)).astype(jnp.bfloat16)
    step = 128 // PADDED * wrows
    target = lax.broadcasted_iota(jnp.int32, (1, 128), 1)
    inside = lax.rem(target, PADDED)
    target = jnp.where(inside < wrows, target // PADDED * wrows + inside, -1)
    row = lax.broadcasted_iota(jnp.int32, (step, 1), 0)
    cut = jnp.where(row == target, 1.0, 0.0).astype(jnp.bfloat16)
    for d, out_ref in zip(steps, out_refs):
        at = pl.multiple_of(lax.rem(x + 4 - d, 4) * columns, columns)
        part = lax.dot_general(
            n_ref[:, pl.ds(at, columns)],
            scaled,
            (((0,), (0,)), ((), ())),
            preferred_element_type=jnp.float32,
        ).astype(jnp.bfloat16)
        for j in range(columns // 128):
            out_ref[j * step : (j + 1) * step, :] = jnp.dot(
                cut, part[j * 128 : (j + 1) * 128], preferred_element_type=jnp.float32
            ).astype(jnp.bfloat16)


def gradient(here, n_all, own, back, wrows, steps):
    shape = jax.ShapeDtypeStruct((n_all.shape[1] // 4 // PADDED * wrows, HALF), jnp.bfloat16)

    def body(*refs):
        gradient_kernel(*refs, steps=steps)

    return pl.pallas_call(
        body,
        out_shape=(shape,) * len(steps),
        in_specs=[SMEM, VMEM, VMEM, VMEM],
        out_specs=(VMEM,) * len(steps),
        compiler_params=pltpu.CompilerParams(vmem_limit_bytes=16 << 20),
        name="gradient",
    )(here, n_all, own, back)


def partner(x, axis):
    return lax.ppermute(x, axis, [(0, 1), (1, 0)])


def from_next(x, axis, distance):
    size = SIZES[AXES.index(axis)]
    return lax.ppermute(x, axis, [((i + distance) % size, i) for i in range(size)])


def local(student_in, weight, queries, keys, values, lengths, assignment):
    names = ("z", "yhi", "core", "ylo", "x")
    here = jnp.stack([lax.axis_index(a) for a in names]).astype(jnp.int32)
    wrows = weight.shape[0]

    lane = lax.broadcasted_iota(jnp.int32, (keys.shape[0], 2 * HD), 1)
    kv = jnp.where(
        lane < HD, jnp.pad(keys, ((0, 0), (0, HD))), jnp.pad(values, ((0, 0), (HD, 0)))
    )
    w_mine, w_other = halves(weight, here[3])
    kv_other = partner(kv, "yhi")
    w_parts = [
        w_mine,
        partner(w_other, "ylo"),
        partner(w_mine, "yhi"),
        lax.ppermute(w_other, ("ylo", "yhi"), [(i, 3 - i) for i in range(4)]),
    ]
    packed = pack(kv, kv_other, w_parts)

    student_in, _ = lax.optimization_barrier((student_in, packed))
    n_keep, n_send = normalise(here, student_in, wrows)
    up, down = from_next(packed, "z", 1), from_next(packed, "z", -1)
    up, down, n_keep, n_send = lax.optimization_barrier((up, down, n_keep, n_send))
    n_got, n_across = partner(n_send, "core"), partner(n_keep, "ylo")

    held = {0: packed, 1: up, -1: down}
    for d in range(2, 5):
        held[d] = from_next(held[d - 1], "z", 1)
        if d < 4:
            held[-d] = from_next(held[1 - d], "z", -1)
        if d == 3:
            held[3], n_got = lax.optimization_barrier((held[3], n_got))
    n_all = jnp.concatenate([n_keep, n_got, n_across, partner(n_got, "ylo")], axis=0)
    parts = [held[d] for d in RING]
    w_rows = jnp.concatenate([part[2 * BLK :] for part in parts], axis=0)
    w_sent = {d: from_next(w_rows, "x", d) for d in (2, 1, 3)}
    w_all = [w_rows] + [w_sent[d] for d in range(1, 4)]

    parts, _ = lax.optimization_barrier((parts, (w_rows, n_across)))
    attention, a_mine, a_other = attend(here, queries, parts, lengths, assignment)

    own, send = project(here, n_all, a_mine, partner(a_other, "ylo"), w_all)
    back = partner(send, "core")
    far, left = gradient(here, n_all, own, back, wrows, (2, 3))
    arrived = [from_next(left, "x", 3), from_next(far, "x", 2)]
    back, _ = lax.optimization_barrier((back, far))
    near, right = gradient(here, n_all, own, back, wrows, (0, 1))
    arrived.append(from_next(right, "x", 1))
    near = near.astype(jnp.float32)
    for block in arrived:
        near = near + block.astype(jnp.float32)
    near = near.astype(jnp.bfloat16).reshape(-1, wrows, HALF)
    near = jnp.pad(near, ((0, 0), (0, PADDED - wrows), (0, 0)))
    last = lax.all_to_all(near, ("ylo", *SEQ), split_axis=0, concat_axis=0, tiled=True)
    summed = last.reshape(2, 16, PADDED, HALF).astype(jnp.float32).sum(axis=1)
    weight_grad = jnp.concatenate([summed[0, :wrows], summed[1, :wrows]], axis=1)
    return (attention, weight_grad)


def solution(mesh):
    mesh = Mesh(mesh.devices.reshape(SIZES), AXES)
    token = P(AXES, None)
    row = P(("ylo", "x", "core"), None)
    return jax.shard_map(
        local,
        mesh=mesh,
        in_specs=(token, token, token, token, token, row, row),
        out_specs=(token, token),
        check_vma=False,
    )
```

```python
import math

import jax
import jax.numpy as jnp
from jax import lax
from jax.experimental import pallas as pl
from jax.experimental.pallas import tpu as pltpu
from jax.sharding import Mesh, PartitionSpec as P

HD = 128
HQ = 4
BLK = 128
COLS = HQ * HD
HALF = COLS // 2
TOKENS_ALL = 32768
PADDED = 16

EPSILON = 1e-06
NEGATIVE = -1e30
LOG2E = math.log2(math.e)

AXES = ("ylo", "x", "core", "z", "yhi")
SIZES = (2, 4, 2, 8, 2)
SEQ = ("z", "yhi")

RING = (0, 1, -1, 2, -2, 3, -3, 4)

SMEM = pl.BlockSpec(memory_space=pltpu.SMEM)
VMEM = pl.BlockSpec(memory_space=pltpu.VMEM)


def spread_tile(first, last, wide, wrows):
    target = lax.broadcasted_iota(jnp.int32, (1, wide), 1)
    inside = lax.rem(target, PADDED)
    target = jnp.where(inside < wrows, target // PADDED * wrows + inside, -1)
    source = lax.broadcasted_iota(jnp.int32, (last - first, 1), 0) + first
    return jnp.where(source == target, 1.0, 0.0).astype(jnp.bfloat16)


def normalise_kernel(where_ref, student_ref, keep_ref, send_ref, *, wrows):
    core = where_ref[2]
    rows, features = student_ref.shape
    group = 16 * PADDED
    taken = 16 * wrows
    chunk = features // 4
    as_float = student_ref[...].astype(jnp.float32)
    scale = lax.rsqrt(jnp.mean(as_float * as_float, axis=1, keepdims=True) + EPSILON)
    normed = (as_float * scale).astype(jnp.bfloat16)
    stacked = jnp.concatenate([normed[:, k * chunk : (k + 1) * chunk] for k in range(4)], axis=0)
    for q in range(chunk // taken):
        first = q * taken // 128 * 128
        last = min(chunk, -(-(q + 1) * taken // 128) * 128)
        tile = spread_tile(first - q * taken, last - q * taken, group, wrows)
        apart = jnp.dot(
            stacked[:, first:last], tile, preferred_element_type=jnp.float32
        ).astype(jnp.bfloat16)
        for k in range(4):
            g = k * (chunk // taken) + q
            at = (g // 2 % 4 * 2 + g // 8) * group
            piece = apart[k * rows : (k + 1) * rows]

            @pl.when(core == g % 2)
            def _():
                keep_ref[:, at : at + group] = piece

            @pl.when(core != g % 2)
            def _():
                send_ref[:, at : at + group] = piece


def normalise(here, student_in, wrows):
    rows, features = student_in.shape
    shape = jax.ShapeDtypeStruct((rows, features // wrows * PADDED // 2), jnp.bfloat16)

    def body(*refs):
        normalise_kernel(*refs, wrows=wrows)

    return pl.pallas_call(
        body,
        out_shape=(shape, shape),
        in_specs=[SMEM, VMEM],
        out_specs=(VMEM, VMEM),
        compiler_params=pltpu.CompilerParams(vmem_limit_bytes=16 << 20),
        name="normalise",
    )(here, student_in)


def pack_kernel(kv_ref, kv_other_ref, *refs):
    *w_refs, out_ref = refs
    rows = kv_ref.shape[0]
    wrows, width = w_refs[0].shape
    out_ref[:rows, :] = kv_ref[...]
    out_ref[rows : 2 * rows, :] = kv_other_ref[...]
    for i, w_ref in enumerate(w_refs):
        first = 2 * rows + i * PADDED
        out_ref[first : first + PADDED, :] = jnp.concatenate(
            [w_ref[...], jnp.zeros((PADDED - wrows, width), jnp.bfloat16)], axis=0
        )


def pack(kv, kv_other, w_parts):
    rows = 2 * kv.shape[0] + len(w_parts) * PADDED
    return pl.pallas_call(
        pack_kernel,
        out_shape=jax.ShapeDtypeStruct((rows, kv.shape[1]), jnp.bfloat16),
        in_specs=[VMEM] * (2 + len(w_parts)),
        out_specs=VMEM,
        compiler_params=pltpu.CompilerParams(vmem_limit_bytes=4 << 20),
        name="pack",
    )(kv, kv_other, *w_parts)


def attend_kernel(where_ref, assign_ref, length_ref, q_ref, *refs):
    *kv_refs, out_ref, mine_ref, other_ref, s_ref = refs
    z, yhi, ylo = where_ref[0], where_ref[1], where_ref[3]
    rows = q_ref.shape[0]
    own = assign_ref[0, 2 * z + yhi] * BLK
    first = length_ref[0, 0]
    second = first + length_ref[0, 1]
    third = second + length_ref[0, 2]
    q_pos = own + lax.broadcasted_iota(jnp.int32, (rows, 1), 0)
    q_start = jnp.where(
        q_pos >= third,
        third,
        jnp.where(q_pos >= second, second, jnp.where(q_pos >= first, first, 0)),
    )
    q_all = jnp.concatenate([q_ref[:, h * HD : (h + 1) * HD] for h in range(HQ)], axis=0)
    lane = lax.broadcasted_iota(jnp.int32, (1, BLK), 1)
    chunk = 2 * BLK
    top = None
    for c, (distance, kv_ref) in enumerate(zip(RING, kv_refs)):
        pair = lax.rem(z + distance + 8, 8) * 2
        k_pos = [assign_ref[0, pair + yhi] * BLK + lane, assign_ref[0, pair + 1 - yhi] * BLK + lane]
        k_pos = jnp.concatenate(k_pos, axis=1)
        bias = jnp.where((k_pos >= q_start) & (k_pos <= q_pos), 0.0, NEGATIVE)
        scores = lax.dot_general(
            q_all,
            kv_ref[:chunk, :HD],
            (((1,), (1,)), ((), ())),
            preferred_element_type=jnp.float32,
        )
        scores = scores.reshape(HQ, rows, chunk) * (HD ** (-0.5) * LOG2E) + bias[None]
        scores = scores.reshape(HQ * rows, chunk)
        s_ref[:, c * chunk : (c + 1) * chunk] = scores
        best = jnp.max(scores, axis=1, keepdims=True)
        top = best if top is None else jnp.maximum(top, best)
    total = jnp.zeros((HQ * rows, 1), jnp.float32)
    mixture = jnp.zeros((HQ * rows, HD), jnp.float32)
    for c, kv_ref in enumerate(kv_refs):
        terms = jnp.exp2(s_ref[:, c * chunk : (c + 1) * chunk] - top)
        total = total + jnp.sum(terms, axis=1, keepdims=True)
        mixture = mixture + jnp.dot(
            terms.astype(jnp.bfloat16), kv_ref[:chunk, HD:], preferred_element_type=jnp.float32
        )
    result = (mixture / total).astype(jnp.bfloat16)
    for h in range(HQ):
        head = result[h * rows : (h + 1) * rows]
        out_ref[:, h * HD : (h + 1) * HD] = head
        at = h % (HQ // 2) * HD

        @pl.when(ylo == h // (HQ // 2))
        def _():
            mine_ref[:, at : at + HD] = head

        @pl.when(ylo != h // (HQ // 2))
        def _():
            other_ref[:, at : at + HD] = head


def attend(here, queries, parts, lengths, assignment):
    rows = queries.shape[0]
    half = jax.ShapeDtypeStruct((rows, HALF), jnp.bfloat16)
    return pl.pallas_call(
        attend_kernel,
        out_shape=(jax.ShapeDtypeStruct((rows, COLS), jnp.bfloat16), half, half),
        in_specs=[SMEM, SMEM, SMEM, VMEM] + [VMEM] * len(parts),
        out_specs=(VMEM, VMEM, VMEM),
        scratch_shapes=[pltpu.VMEM((HQ * rows, 16 * BLK), jnp.float32)],
        compiler_params=pltpu.CompilerParams(vmem_limit_bytes=20 << 20),
        name="attend",
    )(here, assignment, lengths, queries, *parts)


def project_kernel(where_ref, n_ref, mine_ref, got_ref, *refs):
    *w_refs, own_ref, send_ref, w_all = refs
    z, yhi, ylo, x = where_ref[0], where_ref[1], where_ref[3], where_ref[4]
    group = 16 * PADDED
    for d in range(4):
        at_x = lax.rem(x + d, 4) * 2
        for k, distance in enumerate(RING):
            pair = lax.rem(z + distance + 8, 8) * 2
            for t in range(2):
                slot = pair + (yhi if t == 0 else 1 - yhi)
                for i in range(2):
                    side = ylo if i == 0 else 1 - ylo
                    at = (at_x + side) * group + slot * PADDED
                    first = (k * 4 + t * 2 + i) * PADDED
                    w_all[pl.ds(pl.multiple_of(at, PADDED), PADDED), :] = w_refs[d][
                        first : first + PADDED, :
                    ]
    rows = n_ref.shape[0] // 4
    for b in range(4):
        part = jnp.dot(
            n_ref[b * rows : (b + 1) * rows, :], w_all[...], preferred_element_type=jnp.float32
        )
        if b % 2 == 0:
            part = part - (mine_ref, got_ref)[b // 2][...].astype(jnp.float32)
        own_ref[b * rows : (b + 1) * rows, :] = part
        t = b ^ 1
        send_ref[t * rows : (t + 1) * rows, :] = part.astype(jnp.bfloat16)


def project(here, n_all, a_mine, a_got, w_parts):
    shape = (n_all.shape[0], HALF)
    return pl.pallas_call(
        project_kernel,
        out_shape=(
            jax.ShapeDtypeStruct(shape, jnp.float32),
            jax.ShapeDtypeStruct(shape, jnp.bfloat16),
        ),
        in_specs=[SMEM] + [VMEM] * (3 + len(w_parts)),
        out_specs=(VMEM, VMEM),
        scratch_shapes=[pltpu.VMEM((n_all.shape[1], HALF), jnp.bfloat16)],
        compiler_params=pltpu.CompilerParams(vmem_limit_bytes=12 << 20),
        name="project",
    )(here, n_all, a_mine, a_got, *w_parts)


def halves(x, which):
    half = x.shape[1] // 2
    low, high = x[:, :half], x[:, half:]
    return jnp.where(which == 0, low, high), jnp.where(which == 0, high, low)


def gradient_kernel(where_ref, n_ref, own_ref, back_ref, *out_refs, steps):
    x = where_ref[4]
    columns = n_ref.shape[1] // 4
    taken = out_refs[0].shape[0]
    wrows = taken * PADDED // columns
    diff = own_ref[...] + back_ref[...].astype(jnp.float32)
    scaled = (diff * TOKENS_ALL ** (-0.5)).astype(jnp.bfloat16)
    step = 128 // PADDED * wrows
    target = lax.broadcasted_iota(jnp.int32, (1, 128), 1)
    inside = lax.rem(target, PADDED)
    target = jnp.where(inside < wrows, target // PADDED * wrows + inside, -1)
    row = lax.broadcasted_iota(jnp.int32, (step, 1), 0)
    cut = jnp.where(row == target, 1.0, 0.0).astype(jnp.bfloat16)
    for d, out_ref in zip(steps, out_refs):
        at = pl.multiple_of(lax.rem(x + 4 - d, 4) * columns, columns)
        part = lax.dot_general(
            n_ref[:, pl.ds(at, columns)],
            scaled,
            (((0,), (0,)), ((), ())),
            preferred_element_type=jnp.float32,
        ).astype(jnp.bfloat16)
        for j in range(columns // 128):
            out_ref[j * step : (j + 1) * step, :] = jnp.dot(
                cut, part[j * 128 : (j + 1) * 128], preferred_element_type=jnp.float32
            ).astype(jnp.bfloat16)


def gradient(here, n_all, own, back, wrows, steps):
    shape = jax.ShapeDtypeStruct((n_all.shape[1] // 4 // PADDED * wrows, HALF), jnp.bfloat16)

    def body(*refs):
        gradient_kernel(*refs, steps=steps)

    return pl.pallas_call(
        body,
        out_shape=(shape,) * len(steps),
        in_specs=[SMEM, VMEM, VMEM, VMEM],
        out_specs=(VMEM,) * len(steps),
        compiler_params=pltpu.CompilerParams(vmem_limit_bytes=16 << 20),
        name="gradient",
    )(here, n_all, own, back)


def partner(x, axis):
    return lax.ppermute(x, axis, [(0, 1), (1, 0)])


def from_next(x, axis, distance):
    size = SIZES[AXES.index(axis)]
    return lax.ppermute(x, axis, [((i + distance) % size, i) for i in range(size)])


def local(student_in, weight, queries, keys, values, lengths, assignment):
    names = ("z", "yhi", "core", "ylo", "x")
    here = jnp.stack([lax.axis_index(a) for a in names]).astype(jnp.int32)
    wrows = weight.shape[0]

    lane = lax.broadcasted_iota(jnp.int32, (keys.shape[0], 2 * HD), 1)
    kv = jnp.where(
        lane < HD, jnp.pad(keys, ((0, 0), (0, HD))), jnp.pad(values, ((0, 0), (HD, 0)))
    )
    w_mine, w_other = halves(weight, here[3])
    kv_other = partner(kv, "yhi")
    w_parts = [
        w_mine,
        partner(w_other, "ylo"),
        partner(w_mine, "yhi"),
        lax.ppermute(w_other, ("ylo", "yhi"), [(i, 3 - i) for i in range(4)]),
    ]
    packed = pack(kv, kv_other, w_parts)

    student_in, _ = lax.optimization_barrier((student_in, packed))
    n_keep, n_send = normalise(here, student_in, wrows)
    up, down = from_next(packed, "z", 1), from_next(packed, "z", -1)
    up, down, n_keep, n_send = lax.optimization_barrier((up, down, n_keep, n_send))
    n_across = partner(n_keep, "ylo")

    held = {0: packed, 1: up, -1: down}
    for d in range(2, 5):
        held[d] = from_next(held[d - 1], "z", 1)
        if d < 4:
            held[-d] = from_next(held[1 - d], "z", -1)
        if d == 2:
            n_sent, _ = lax.optimization_barrier((n_send, held[2]))
            n_diag = lax.ppermute(n_sent, ("ylo", "core"), [(i, 3 - i) for i in range(4)])
    n_late, _ = lax.optimization_barrier((n_send, held[4]))
    n_got = partner(n_late, "core")
    n_all = jnp.concatenate([n_keep, n_got, n_across, n_diag], axis=0)
    parts = [held[d] for d in RING]
    w_rows = jnp.concatenate([part[2 * BLK :] for part in parts], axis=0)
    w_sent = {d: from_next(w_rows, "x", d) for d in (2, 1, 3)}
    w_all = [w_rows] + [w_sent[d] for d in range(1, 4)]

    parts, _ = lax.optimization_barrier((parts, (w_rows, n_across)))
    attention, a_mine, a_other = attend(here, queries, parts, lengths, assignment)

    own, send = project(here, n_all, a_mine, partner(a_other, "ylo"), w_all)
    back = partner(send, "core")
    far, left = gradient(here, n_all, own, back, wrows, (2, 3))
    arrived = [from_next(left, "x", 3), from_next(far, "x", 2)]
    back, _ = lax.optimization_barrier((back, far))
    near, right = gradient(here, n_all, own, back, wrows, (0, 1))
    arrived.append(from_next(right, "x", 1))
    near = near.astype(jnp.float32)
    for block in arrived:
        near = near + block.astype(jnp.float32)
    near = near.astype(jnp.bfloat16).reshape(-1, wrows, HALF)
    near = jnp.pad(near, ((0, 0), (0, PADDED - wrows), (0, 0)))
    last = lax.all_to_all(near, ("ylo", *SEQ), split_axis=0, concat_axis=0, tiled=True)
    summed = last.reshape(2, 16, PADDED, HALF).astype(jnp.float32).sum(axis=1)
    weight_grad = jnp.concatenate([summed[0, :wrows], summed[1, :wrows]], axis=1)
    return (attention, weight_grad)


def solution(mesh):
    mesh = Mesh(mesh.devices.reshape(SIZES), AXES)
    token = P(AXES, None)
    row = P(("ylo", "x", "core"), None)
    return jax.shard_map(
        local,
        mesh=mesh,
        in_specs=(token, token, token, token, token, row, row),
        out_specs=(token, token),
        check_vma=False,
    )
```

```python
import math

import jax
import jax.numpy as jnp
from jax import lax
from jax.experimental import pallas as pl
from jax.experimental.pallas import tpu as pltpu
from jax.sharding import Mesh, PartitionSpec as P

HD = 128
HQ = 4
BLK = 128
COLS = HQ * HD
HALF = COLS // 2
TOKENS_ALL = 32768
PADDED = 16

EPSILON = 1e-06
NEGATIVE = -1e30
LOG2E = math.log2(math.e)

AXES = ("ylo", "x", "core", "z", "yhi")
SIZES = (2, 4, 2, 8, 2)
SEQ = ("z", "yhi")

RING = (0, 1, -1, 2, -2, 3, -3, 4)

SMEM = pl.BlockSpec(memory_space=pltpu.SMEM)
VMEM = pl.BlockSpec(memory_space=pltpu.VMEM)


def spread_tile(first, last, wide, wrows):
    target = lax.broadcasted_iota(jnp.int32, (1, wide), 1)
    inside = lax.rem(target, PADDED)
    target = jnp.where(inside < wrows, target // PADDED * wrows + inside, -1)
    source = lax.broadcasted_iota(jnp.int32, (last - first, 1), 0) + first
    return jnp.where(source == target, 1.0, 0.0).astype(jnp.bfloat16)


def normalise_kernel(where_ref, student_ref, keep_ref, send_ref, *, wrows):
    core = where_ref[2]
    rows, features = student_ref.shape
    group = 16 * PADDED
    taken = 16 * wrows
    chunk = features // 4
    as_float = student_ref[...].astype(jnp.float32)
    scale = lax.rsqrt(jnp.mean(as_float * as_float, axis=1, keepdims=True) + EPSILON)
    normed = (as_float * scale).astype(jnp.bfloat16)
    stacked = jnp.concatenate([normed[:, k * chunk : (k + 1) * chunk] for k in range(4)], axis=0)
    for q in range(chunk // taken):
        first = q * taken // 128 * 128
        last = min(chunk, -(-(q + 1) * taken // 128) * 128)
        tile = spread_tile(first - q * taken, last - q * taken, group, wrows)
        apart = jnp.dot(
            stacked[:, first:last], tile, preferred_element_type=jnp.float32
        ).astype(jnp.bfloat16)
        for k in range(4):
            g = k * (chunk // taken) + q
            at = (g // 2 % 4 * 2 + g // 8) * group
            piece = apart[k * rows : (k + 1) * rows]

            @pl.when(core == g % 2)
            def _():
                keep_ref[:, at : at + group] = piece

            @pl.when(core != g % 2)
            def _():
                send_ref[:, at : at + group] = piece


def normalise(here, student_in, wrows):
    rows, features = student_in.shape
    shape = jax.ShapeDtypeStruct((rows, features // wrows * PADDED // 2), jnp.bfloat16)

    def body(*refs):
        normalise_kernel(*refs, wrows=wrows)

    return pl.pallas_call(
        body,
        out_shape=(shape, shape),
        in_specs=[SMEM, VMEM],
        out_specs=(VMEM, VMEM),
        compiler_params=pltpu.CompilerParams(vmem_limit_bytes=16 << 20),
        name="normalise",
    )(here, student_in)


def pack_kernel(kv_ref, kv_other_ref, *refs):
    *w_refs, out_ref = refs
    rows = kv_ref.shape[0]
    wrows, width = w_refs[0].shape
    out_ref[:rows, :] = kv_ref[...]
    out_ref[rows : 2 * rows, :] = kv_other_ref[...]
    for i, w_ref in enumerate(w_refs):
        first = 2 * rows + i * PADDED
        out_ref[first : first + PADDED, :] = jnp.concatenate(
            [w_ref[...], jnp.zeros((PADDED - wrows, width), jnp.bfloat16)], axis=0
        )


def pack(kv, kv_other, w_parts):
    rows = 2 * kv.shape[0] + len(w_parts) * PADDED
    return pl.pallas_call(
        pack_kernel,
        out_shape=jax.ShapeDtypeStruct((rows, kv.shape[1]), jnp.bfloat16),
        in_specs=[VMEM] * (2 + len(w_parts)),
        out_specs=VMEM,
        compiler_params=pltpu.CompilerParams(vmem_limit_bytes=4 << 20),
        name="pack",
    )(kv, kv_other, *w_parts)


def attend_kernel(where_ref, assign_ref, length_ref, q_ref, *refs):
    *kv_refs, out_ref, mine_ref, other_ref, s_ref = refs
    z, yhi, ylo = where_ref[0], where_ref[1], where_ref[3]
    rows = q_ref.shape[0]
    own = assign_ref[0, 2 * z + yhi] * BLK
    first = length_ref[0, 0]
    second = first + length_ref[0, 1]
    third = second + length_ref[0, 2]
    q_pos = own + lax.broadcasted_iota(jnp.int32, (rows, 1), 0)
    q_start = jnp.where(
        q_pos >= third,
        third,
        jnp.where(q_pos >= second, second, jnp.where(q_pos >= first, first, 0)),
    )
    q_all = jnp.concatenate([q_ref[:, h * HD : (h + 1) * HD] for h in range(HQ)], axis=0)
    lane = lax.broadcasted_iota(jnp.int32, (1, BLK), 1)
    chunk = 2 * BLK
    top = None
    for c, (distance, kv_ref) in enumerate(zip(RING, kv_refs)):
        pair = lax.rem(z + distance + 8, 8) * 2
        k_pos = [assign_ref[0, pair + yhi] * BLK + lane, assign_ref[0, pair + 1 - yhi] * BLK + lane]
        k_pos = jnp.concatenate(k_pos, axis=1)
        bias = jnp.where((k_pos >= q_start) & (k_pos <= q_pos), 0.0, NEGATIVE)
        scores = lax.dot_general(
            q_all,
            kv_ref[:chunk, :HD],
            (((1,), (1,)), ((), ())),
            preferred_element_type=jnp.float32,
        )
        scores = scores.reshape(HQ, rows, chunk) * (HD ** (-0.5) * LOG2E) + bias[None]
        scores = scores.reshape(HQ * rows, chunk)
        s_ref[:, c * chunk : (c + 1) * chunk] = scores
        best = jnp.max(scores, axis=1, keepdims=True)
        top = best if top is None else jnp.maximum(top, best)
    total = jnp.zeros((HQ * rows, 1), jnp.float32)
    mixture = jnp.zeros((HQ * rows, HD), jnp.float32)
    for c, kv_ref in enumerate(kv_refs):
        terms = jnp.exp2(s_ref[:, c * chunk : (c + 1) * chunk] - top)
        total = total + jnp.sum(terms, axis=1, keepdims=True)
        mixture = mixture + jnp.dot(
            terms.astype(jnp.bfloat16), kv_ref[:chunk, HD:], preferred_element_type=jnp.float32
        )
    result = (mixture / total).astype(jnp.bfloat16)
    for h in range(HQ):
        head = result[h * rows : (h + 1) * rows]
        out_ref[:, h * HD : (h + 1) * HD] = head
        at = h % (HQ // 2) * HD

        @pl.when(ylo == h // (HQ // 2))
        def _():
            mine_ref[:, at : at + HD] = head

        @pl.when(ylo != h // (HQ // 2))
        def _():
            other_ref[:, at : at + HD] = head


def attend(here, queries, parts, lengths, assignment):
    rows = queries.shape[0]
    half = jax.ShapeDtypeStruct((rows, HALF), jnp.bfloat16)
    return pl.pallas_call(
        attend_kernel,
        out_shape=(jax.ShapeDtypeStruct((rows, COLS), jnp.bfloat16), half, half),
        in_specs=[SMEM, SMEM, SMEM, VMEM] + [VMEM] * len(parts),
        out_specs=(VMEM, VMEM, VMEM),
        scratch_shapes=[pltpu.VMEM((HQ * rows, 16 * BLK), jnp.float32)],
        compiler_params=pltpu.CompilerParams(vmem_limit_bytes=20 << 20),
        name="attend",
    )(here, assignment, lengths, queries, *parts)


def project_kernel(where_ref, n_ref, mine_ref, got_ref, *refs):
    *w_refs, own_ref, send_ref, w_all = refs
    z, yhi, ylo, x = where_ref[0], where_ref[1], where_ref[3], where_ref[4]
    group = 16 * PADDED
    for d in range(4):
        at_x = lax.rem(x + d, 4) * 2
        for k, distance in enumerate(RING):
            pair = lax.rem(z + distance + 8, 8) * 2
            for t in range(2):
                slot = pair + (yhi if t == 0 else 1 - yhi)
                for i in range(2):
                    side = ylo if i == 0 else 1 - ylo
                    at = (at_x + side) * group + slot * PADDED
                    first = (k * 4 + t * 2 + i) * PADDED
                    w_all[pl.ds(pl.multiple_of(at, PADDED), PADDED), :] = w_refs[d][
                        first : first + PADDED, :
                    ]
    rows = n_ref.shape[0] // 4
    for b in range(4):
        part = jnp.dot(
            n_ref[b * rows : (b + 1) * rows, :], w_all[...], preferred_element_type=jnp.float32
        )
        if b % 2 == 0:
            part = part - (mine_ref, got_ref)[b // 2][...].astype(jnp.float32)
        own_ref[b * rows : (b + 1) * rows, :] = part
        t = b ^ 1
        send_ref[t * rows : (t + 1) * rows, :] = part.astype(jnp.bfloat16)


def project(here, n_all, a_mine, a_got, w_parts):
    shape = (n_all.shape[0], HALF)
    return pl.pallas_call(
        project_kernel,
        out_shape=(
            jax.ShapeDtypeStruct(shape, jnp.float32),
            jax.ShapeDtypeStruct(shape, jnp.bfloat16),
        ),
        in_specs=[SMEM] + [VMEM] * (3 + len(w_parts)),
        out_specs=(VMEM, VMEM),
        scratch_shapes=[pltpu.VMEM((n_all.shape[1], HALF), jnp.bfloat16)],
        compiler_params=pltpu.CompilerParams(vmem_limit_bytes=12 << 20),
        name="project",
    )(here, n_all, a_mine, a_got, *w_parts)


def halves(x, which):
    half = x.shape[1] // 2
    low, high = x[:, :half], x[:, half:]
    return jnp.where(which == 0, low, high), jnp.where(which == 0, high, low)


def gradient_kernel(where_ref, n_ref, own_ref, back_ref, *out_refs, steps):
    x = where_ref[4]
    columns = n_ref.shape[1] // 4
    taken = out_refs[0].shape[0]
    wrows = taken * PADDED // columns
    diff = own_ref[...] + back_ref[...].astype(jnp.float32)
    scaled = (diff * TOKENS_ALL ** (-0.5)).astype(jnp.bfloat16)
    step = 128 // PADDED * wrows
    target = lax.broadcasted_iota(jnp.int32, (1, 128), 1)
    inside = lax.rem(target, PADDED)
    target = jnp.where(inside < wrows, target // PADDED * wrows + inside, -1)
    row = lax.broadcasted_iota(jnp.int32, (step, 1), 0)
    cut = jnp.where(row == target, 1.0, 0.0).astype(jnp.bfloat16)
    for d, out_ref in zip(steps, out_refs):
        at = pl.multiple_of(lax.rem(x + 4 - d, 4) * columns, columns)
        part = lax.dot_general(
            n_ref[:, pl.ds(at, columns)],
            scaled,
            (((0,), (0,)), ((), ())),
            preferred_element_type=jnp.float32,
        ).astype(jnp.bfloat16)
        for j in range(columns // 128):
            out_ref[j * step : (j + 1) * step, :] = jnp.dot(
                cut, part[j * 128 : (j + 1) * 128], preferred_element_type=jnp.float32
            ).astype(jnp.bfloat16)


def gradient(here, n_all, own, back, wrows, steps):
    shape = jax.ShapeDtypeStruct((n_all.shape[1] // 4 // PADDED * wrows, HALF), jnp.bfloat16)

    def body(*refs):
        gradient_kernel(*refs, steps=steps)

    return pl.pallas_call(
        body,
        out_shape=(shape,) * len(steps),
        in_specs=[SMEM, VMEM, VMEM, VMEM],
        out_specs=(VMEM,) * len(steps),
        compiler_params=pltpu.CompilerParams(vmem_limit_bytes=16 << 20),
        name="gradient",
    )(here, n_all, own, back)


def partner(x, axis):
    return lax.ppermute(x, axis, [(0, 1), (1, 0)])


def from_next(x, axis, distance):
    size = SIZES[AXES.index(axis)]
    return lax.ppermute(x, axis, [((i + distance) % size, i) for i in range(size)])


def local(student_in, weight, queries, keys, values, lengths, assignment):
    names = ("z", "yhi", "core", "ylo", "x")
    here = jnp.stack([lax.axis_index(a) for a in names]).astype(jnp.int32)
    wrows = weight.shape[0]

    lane = lax.broadcasted_iota(jnp.int32, (keys.shape[0], 2 * HD), 1)
    kv = jnp.where(
        lane < HD, jnp.pad(keys, ((0, 0), (0, HD))), jnp.pad(values, ((0, 0), (HD, 0)))
    )
    w_mine, w_other = halves(weight, here[3])
    kv_other = partner(kv, "yhi")
    w_parts = [
        w_mine,
        partner(w_other, "ylo"),
        partner(w_mine, "yhi"),
        lax.ppermute(w_other, ("ylo", "yhi"), [(i, 3 - i) for i in range(4)]),
    ]
    packed = pack(kv, kv_other, w_parts)

    student_in, _ = lax.optimization_barrier((student_in, packed))
    n_keep, n_send = normalise(here, student_in, wrows)
    up, down = from_next(packed, "z", 1), from_next(packed, "z", -1)
    up, down, n_keep, n_send = lax.optimization_barrier((up, down, n_keep, n_send))
    n_got, n_across = partner(n_send, "core"), partner(n_keep, "ylo")

    held = {0: packed, 1: up, -1: down}
    for d in range(2, 5):
        held[d] = from_next(held[d - 1], "z", 1)
        if d < 4:
            held[-d] = from_next(held[1 - d], "z", -1)
        if d == 3:
            held[3], n_got = lax.optimization_barrier((held[3], n_got))
    n_all = jnp.concatenate([n_keep, n_got, n_across, partner(n_got, "ylo")], axis=0)
    parts = [held[d] for d in RING]
    w_rows = jnp.concatenate([part[2 * BLK :] for part in parts], axis=0)
    w_sent = {d: from_next(w_rows, "x", d) for d in (2, 1, 3)}
    w_all = [w_rows] + [w_sent[d] for d in range(1, 4)]

    parts, _ = lax.optimization_barrier((parts, (w_rows, n_across)))
    attention, a_mine, a_other = attend(here, queries, parts, lengths, assignment)

    own, send = project(here, n_all, a_mine, partner(a_other, "ylo"), w_all)
    back = partner(send, "core")
    (far,) = gradient(here, n_all, own, back, wrows, (2,))
    arrived = [from_next(far, "x", 2)]
    back, _ = lax.optimization_barrier((back, far))
    near, right, left = gradient(here, n_all, own, back, wrows, (0, 1, 3))
    arrived += [from_next(left, "x", 3), from_next(right, "x", 1)]
    near = near.astype(jnp.float32)
    for block in arrived:
        near = near + block.astype(jnp.float32)
    near = near.astype(jnp.bfloat16).reshape(-1, wrows, HALF)
    near = jnp.pad(near, ((0, 0), (0, PADDED - wrows), (0, 0)))
    last = lax.all_to_all(near, ("ylo", *SEQ), split_axis=0, concat_axis=0, tiled=True)
    summed = last.reshape(2, 16, PADDED, HALF).astype(jnp.float32).sum(axis=1)
    weight_grad = jnp.concatenate([summed[0, :wrows], summed[1, :wrows]], axis=1)
    return (attention, weight_grad)


def solution(mesh):
    mesh = Mesh(mesh.devices.reshape(SIZES), AXES)
    token = P(AXES, None)
    row = P(("ylo", "x", "core"), None)
    return jax.shard_map(
        local,
        mesh=mesh,
        in_specs=(token, token, token, token, token, row, row),
        out_specs=(token, token),
        check_vma=False,
    )
```
